256 devices in a mesh: ent: 64 (over x, y, z_hi), rel: 4 (over z_lo, core).
Axes of the slice: x: 4, y: 4, z: 8 (z_hi: 4, z_lo: 2; z = z_hi * 2 + z_lo), core: 2. Of those that a mesh axis runs over, the one named last changes fastest.
Arguments:
- entity_table: bfloat16 [1024, 1024], P('ent'), may hold values from -1.5 to 1.5
- phases: float32 [4096, 512], P('rel'), may hold values from -3.140625 to 3.140625
- head_owner: int32 [131072, 1], P(('ent', 'rel')), may hold values from 0 to 255; in each aligned block of 512 rows (0 to 511, 512 to 1023, ...) at most 4 rows name the same one
- head_row: int32 [131072], P(('ent', 'rel')), may hold values from 0 to 3
- relation: int32 [131072], P(('ent', 'rel')), may hold values from 0 to 1023
- tail_ids: int32 [131072], P(('ent', 'rel')), may hold values from 0 to 1023
- known_tails: int32 [131072, 32], P(('ent', 'rel')), may hold values from 0 to 1023
Outputs:
- entity_gradient: float32 [1024, 1024], P(('ent', 'rel'))
- relation_gradient: float32 [4096, 512], P('rel')
The draws below stay inside these ranges and needn't reach their ends.
Inputs may be any that keep to these rules, and one draw needn't show every extreme that they name: `head_owner`: owner o of the 256 holds working-set rows o * 4 to o * 4 + 3 and is device (o // 4, o mod 4) of ent and rel. Among the 512 triples of one device at most 4 have heads held by one owner, and exactly 4 in some devices. The triples of block b of 512 belong to relation group b mod 4.
All inputs are finite; a program needn't handle non-finite values.
Results may differ from the reference program's by a relative error of at most 0.004.
Values may be sent and summed in bfloat16 or wider, within the bound.
A program may use at most 64 MiB of HBM per device.

```python
import math
import jax
import jax.numpy as jnp
import numpy as np
from jax import lax

DIM = 512
WIDTH = 1024
RELS = 4096
LISTED = 32
TRIP_DEV = 512
OWNERS = 256
ENTITIES = 1024
TRIPLES = 131072
REL_GRP = 1024
ROWS_OWN = 4
CAP = 4
N_REL = 4


def draw_entity_table(key, part):
    key_base, key_scale = jax.random.split(jax.random.fold_in(key, 11), 2)
    spread = jnp.exp(jax.random.uniform(key_scale, (ENTITIES, 1), jnp.float32, 0.0, math.log(1.5)))
    base = jnp.clip(jax.random.normal(key_base, (ENTITIES, WIDTH), jnp.float32), -5.0, 5.0)
    return (0.045 * base * spread).astype(jnp.bfloat16)


def plant(entries, own_key, smallest, top_value):
    longest = entries.shape.index(max(entries.shape))
    spots = []
    for shift in (0, 1):
        where = [jax.random.randint(jax.random.fold_in(own_key, axis), (), 0, length) for axis, length in enumerate(entries.shape)]
        where[longest] = (where[longest] + shift) % entries.shape[longest]
        spots.append(tuple(where))
    return entries.at[spots[0]].set(smallest).at[spots[1]].set(top_value)


def rank_bounds(amount, skew):
    loads = [(1 << 20) // math.isqrt(grade ** skew) + 1 for grade in range(1, amount + 1)]
    width = 1 + sum(loads) // (1 << 30)
    return np.cumsum(np.array([max(1, weight // width) for weight in loads]))


def ranked_ids(own_key, dims, count, slope):
    table = rank_bounds(count, slope)
    lot = jax.random.randint(jax.random.fold_in(own_key, 1), dims, 0, int(table[count - 1]))
    rank = jnp.searchsorted(jnp.asarray(table, jnp.int32), lot, side="right")
    return jax.random.permutation(jax.random.fold_in(own_key, 2), count)[rank].astype(jnp.int32)


def routed_block(key, own, number, rows, count, top, limit, lean):
    ranking = jax.random.permutation(key, count)
    crowded, usual = portions_of(count, rows * top, limit, lean, True), portions_of(count, rows * top, limit, lean, False)
    places = jnp.arange(count)

    def named(tallies, rotation):
        used = int((tallies > 0).sum())
        fixed = max(1, used // 4)
        shifted = fixed + (places - fixed + rotation * (used - fixed)) % max(1, count - fixed)
        return jnp.zeros((count,), jnp.int32).at[ranking[jnp.where(places < fixed, places, shifted)]].set(jnp.asarray(tallies, jnp.int32))

    tallies = jnp.where(number % 4 == 0, named(crowded, number // 4), named(usual, number - number // 4 - 1))
    mixed = jax.random.permutation(jax.random.fold_in(own, 3), count)
    giver, sink = mixed[0:count // 2 * 2:2], mixed[1:count // 2 * 2:2]
    room = jnp.minimum(tallies[giver] - 1, limit - tallies[sink]) // 2
    room = jnp.where((giver == ranking[0]) | (sink == ranking[0]) | (tallies[sink] == 0), 0, jnp.maximum(room, 0))
    shifted = jax.random.randint(jax.random.fold_in(own, 4), (count // 2,), 0, 1 << 20) % (room + 1)
    tallies = tallies.at[giver].add(-shifted).at[sink].add(shifted)
    labels = jnp.searchsorted(jnp.cumsum(tallies), jnp.arange(rows * top), side="right").astype(jnp.int32)
    listing = labels.reshape(top, rows).T
    listing = listing[jax.random.permutation(jax.random.fold_in(own, 1), rows)]
    rotation = jax.random.randint(jax.random.fold_in(own, 2), (rows, 1), 0, top)
    return jnp.take_along_axis(listing, (jnp.arange(top)[None, :] + rotation) % top, axis=1)


def portions_of(number_of, total, limit, slope, full):
    loads = [(1 << 20) // math.isqrt(grade ** slope) + 1 for grade in range(1, number_of + 1)]
    largest = limit if full else min(limit, max(-(-total // number_of), total * loads[0] // sum(loads)))
    least = 1 if total - largest >= number_of - 1 else 0
    given, surplus = [largest] + [least] * (number_of - 1), total - largest - least * (number_of - 1)
    while surplus > 0:
        candidates = [i for i in range(1, number_of) if given[i] < largest] or [i for i in range(1, number_of) if given[i] < limit]
        whole, left = sum([loads[i] for i in candidates]), surplus
        for i in candidates:
            extra = min(limit - given[i], max(1, left * loads[i] // whole), surplus)
            given[i] = given[i] + extra
            surplus = surplus - extra
    return np.array(given)


def setup_inputs(seed: int = 0) -> dict:
    key_of = jax.random.split(jax.random.key(seed), 8)
    entity_table = draw_entity_table(jax.random.fold_in(key_of[7], 71), 0)
    phases = jnp.clip(jax.random.uniform(key_of[1], (RELS, DIM), jnp.float32, -3.140625, 3.140625), -3.140625, 3.140625)
    head_owner_keys = jax.random.split(jax.random.fold_in(key_of[2], 1), TRIPLES // TRIP_DEV)
    head_owner_turns = jax.random.permutation(jax.random.fold_in(key_of[2], 3), TRIPLES // TRIP_DEV)
    head_owner = jax.vmap(lambda own, number: routed_block(jax.random.fold_in(key_of[2], 2), own, number, TRIP_DEV, OWNERS, 1, CAP, 2))(head_owner_keys, head_owner_turns).reshape((TRIPLES, 1))
    head_row = plant(ranked_ids(key_of[3], (TRIPLES,), ROWS_OWN, 2), jax.random.fold_in(key_of[3], 3), 0, ROWS_OWN - 1).astype(jnp.int32)
    relation = plant(jax.random.randint(key_of[4], (TRIPLES,), 0, REL_GRP), jax.random.fold_in(key_of[4], 1), 0, REL_GRP - 1).astype(jnp.int32)
    tail_ids = plant(jax.random.randint(key_of[5], (TRIPLES,), 0, ENTITIES), jax.random.fold_in(key_of[5], 1), 0, ENTITIES - 1).astype(jnp.int32)
    known_tails = plant(jax.random.randint(key_of[6], (TRIPLES, LISTED), 0, ENTITIES), jax.random.fold_in(key_of[6], 1), 0, ENTITIES - 1).astype(jnp.int32)
    return {"entity_table": entity_table, "phases": phases, "head_owner": head_owner, "head_row": head_row, "relation": relation, "tail_ids": tail_ids, "known_tails": known_tails}


def reference(entity_table, phases, head_owner, head_row, relation, tail_ids, known_tails):
    table_f = entity_table.astype(jnp.float32)
    table_sq = jnp.sum(table_f * table_f, axis=1)
    columns = jnp.arange(ENTITIES, dtype=jnp.int32)
    blocks_n = TRIPLES // TRIP_DEV

    def one_block(carry, index_b):
        grad_acc, rel_acc = carry
        start = (index_b * TRIP_DEV).astype(jnp.int32)
        owners = lax.dynamic_slice_in_dim(head_owner[:, 0], start, TRIP_DEV)
        rows_in = lax.dynamic_slice_in_dim(head_row, start, TRIP_DEV)
        rel_local = lax.dynamic_slice_in_dim(relation, start, TRIP_DEV)
        targets = lax.dynamic_slice_in_dim(tail_ids, start, TRIP_DEV)
        listed_ids = lax.dynamic_slice_in_dim(known_tails, start, TRIP_DEV, 0)
        heads = (owners * ROWS_OWN + rows_in).astype(jnp.int32)
        rel_glob = ((index_b % N_REL) * REL_GRP + rel_local).astype(jnp.int32)
        head_f = table_f[heads]
        angles = phases[rel_glob]
        cosine = jnp.cos(angles)
        sine_part = jnp.sin(angles)
        head_re = head_f[:, :DIM]
        head_im = head_f[:, DIM:]
        query_re = head_re * cosine - head_im * sine_part
        query_im = head_re * sine_part + head_im * cosine
        query = jnp.concatenate([query_re, query_im], axis=1).astype(jnp.bfloat16)
        query_f = query.astype(jnp.float32)
        query_sq = jnp.sum(query_f * query_f, axis=1)
        cross = jnp.dot(query, entity_table.T, preferred_element_type=jnp.float32)
        scores = 2.0 * cross - query_sq[:, None] - table_sq[None, :]
        listed = jnp.zeros((TRIP_DEV, ENTITIES), jnp.bool_)
        for column_j in range(LISTED):
            listed = listed | (listed_ids[:, column_j:column_j + 1] == columns[None, :])
        masked = listed & (columns[None, :] != targets[:, None])
        row_max = jnp.max(jnp.where(masked, -jnp.inf, scores), axis=1)
        raw_prob = jnp.where(masked, 0.0, jnp.exp(scores - row_max[:, None]))
        prob = raw_prob / jnp.sum(raw_prob, axis=1, keepdims=True)
        onehot = (columns[None, :] == targets[:, None]).astype(jnp.float32)
        weights = (prob - onehot).astype(jnp.bfloat16)
        dquery = 2.0 * jnp.dot(weights, entity_table, preferred_element_type=jnp.float32)
        grad_re = dquery[:, :DIM]
        grad_im = dquery[:, DIM:]
        head_rows = jnp.concatenate([grad_re * cosine + grad_im * sine_part, -grad_re * sine_part + grad_im * cosine], axis=1).astype(jnp.bfloat16)
        dangle = -query_im * grad_re + query_re * grad_im
        cross_t = lax.dot_general(weights, query, (((0,), (0,)), ((), ())), preferred_element_type=jnp.float32)
        counts = jnp.sum(weights.astype(jnp.float32), axis=0)
        term = 2.0 * (cross_t - counts[:, None] * table_f)
        head_term = jax.ops.segment_sum(head_rows.astype(jnp.float32), heads, num_segments=ENTITIES)
        rel_term = jax.ops.segment_sum(dangle, rel_glob, num_segments=RELS)
        return (grad_acc + term + head_term, rel_acc + rel_term), None

    start_carry = (jnp.zeros((ENTITIES, WIDTH), jnp.float32), jnp.zeros((RELS, DIM), jnp.float32))
    (entity_gradient, relation_gradient), unused = lax.scan(one_block, start_carry, jnp.arange(blocks_n, dtype=jnp.int32))
    return entity_gradient, relation_gradient
```

```python
import functools

import jax
import jax.numpy as jnp
from jax import lax
from jax.experimental import pallas as pl
from jax.experimental.pallas import tpu as pltpu
from jax.sharding import PartitionSpec as P

MESH = pl.DeviceIdType.MESH
VMEM = pltpu.VMEM
F32 = jnp.float32
BF16 = jnp.bfloat16
WIRE = jnp.bfloat16
COLS = 512

SIN = (0.9999999999932018, -0.16666666657817392, 0.008333333144447052, -0.00019841254471923497,
       2.7556704311932283e-06, -2.5038717712098566e-08, 1.5896746642760318e-10, -6.610935072102146e-13)
COS = (0.9999999999990714, -0.4999999999846839, 0.041666666625163704, -0.0013888888455803566,
       2.480156464708791e-05, -2.755665269895137e-07, 2.0865211281170485e-09, -1.1353643820753535e-11,
       4.131574377242709e-14)


def horner(coefficients, t):
    value = jnp.full_like(t, coefficients[-1])
    for c in coefficients[-2::-1]:
        value = value * t + c
    return value


def place():
    e = lax.axis_index("ent")
    r = lax.axis_index("rel")
    return e // 16, (e // 4) % 4, e % 4, r // 2, r % 2


def device(x, y, zh, zl, core):
    return {"ent": x * 16 + y * 4 + zh, "rel": zl * 2 + core}


class Wire:
    def __init__(self, send, recv):
        self.send, self.recv = send, recv
        self.count = 0
        self.open = []

    def number(self):
        self.count += 1
        return self.count - 1

    def start(self, t, src, dst, to):
        copy = pltpu.make_async_remote_copy(
            src_ref=src, dst_ref=dst, send_sem=self.send.at[t], recv_sem=self.recv.at[t],
            device_id=to, device_id_type=MESH)
        copy.start()
        self.open.append(copy)

    def wait(self, t, dst, to):
        pltpu.make_async_remote_copy(
            src_ref=dst, dst_ref=dst, send_sem=self.send.at[t], recv_sem=self.recv.at[t],
            device_id=to, device_id_type=MESH).wait_recv()

    def drain(self):
        for copy in self.open:
            copy.wait_send()
        self.open = []


def greet(x, y, zh, zl, core):
    barrier = pltpu.get_barrier_semaphore()
    z = zh * 2 + zl
    peers = [device(x, y, zh, zl, 1 - core)]
    for d in (1, 3):
        peers.append(device((x + d) % 4, y, zh, zl, core))
        peers.append(device(x, (y + d) % 4, zh, zl, core))
    for d in range(1, 8):
        zz = (z + d) % 8
        peers.append(device(x, y, zz // 2, zz % 2, core))
    for peer in peers:
        pl.semaphore_signal(barrier, inc=1, device_id=peer, device_id_type=MESH)
    pl.semaphore_wait(barrier, len(peers))


class Spread:
    def __init__(self, wire, block, to, a0, b0, have):
        self.w, self.block, self.to, self.a0, self.b0, self.have = wire, block, to, a0, b0, have
        number = wire.number
        self.tb = [number() for _ in range(4)]
        self.ta = [[number() for _ in range(4)] for _ in range(4)]

    def half(self, a, b, h):
        return self.block(a, b).at[pl.ds(32 * h, 32)]

    def got(self, j):
        a0, b = self.a0, (self.b0 + j) % 4
        blk = self.block(a0, b)
        self.w.start(self.ta[j][0], blk, blk, self.to((a0 + 1) % 4, self.b0))
        self.w.start(self.ta[j][1], blk, blk, self.to((a0 + 3) % 4, self.b0))
        self.have(a0, b, j)

    def begin(self):
        a0, b0 = self.a0, self.b0
        blk = self.block(a0, b0)
        self.w.start(self.tb[0], blk, blk, self.to(a0, (b0 + 1) % 4))
        self.w.start(self.tb[1], blk, blk, self.to(a0, (b0 + 3) % 4))
        self.got(0)

    def along_b(self):
        a0, b0, w = self.a0, self.b0, self.w
        up, down = self.to(a0, (b0 + 1) % 4), self.to(a0, (b0 + 3) % 4)
        w.wait(self.tb[0], self.block(a0, (b0 + 3) % 4), down)
        part = self.half(a0, (b0 + 3) % 4, 0)
        w.start(self.tb[2], part, part, up)
        self.got(3)
        w.wait(self.tb[1], self.block(a0, (b0 + 1) % 4), up)
        part = self.half(a0, (b0 + 1) % 4, 1)
        w.start(self.tb[3], part, part, down)
        self.got(1)

    def along_b_far(self):
        a0, b0, w = self.a0, self.b0, self.w
        up, down = self.to(a0, (b0 + 1) % 4), self.to(a0, (b0 + 3) % 4)
        far = (b0 + 2) % 4
        w.wait(self.tb[2], self.half(a0, far, 0), down)
        w.wait(self.tb[3], self.half(a0, far, 1), up)
        self.got(2)

    def along_a(self, j):
        a0, w = self.a0, self.w
        b = (self.b0 + j) % 4
        up, down = self.to((a0 + 1) % 4, self.b0), self.to((a0 + 3) % 4, self.b0)
        t = self.ta[j]
        w.wait(t[0], self.block((a0 + 3) % 4, b), down)
        part = self.half((a0 + 3) % 4, b, 0)
        w.start(t[2], part, part, up)
        self.have((a0 + 3) % 4, b, 4 + j)
        w.wait(t[1], self.block((a0 + 1) % 4, b), up)
        part = self.half((a0 + 1) % 4, b, 1)
        w.start(t[3], part, part, down)
        self.have((a0 + 1) % 4, b, 8 + j)

    def along_a_far(self, j):
        a0, w = self.a0, self.w
        b = (self.b0 + j) % 4
        up, down = self.to((a0 + 1) % 4, self.b0), self.to((a0 + 3) % 4, self.b0)
        t = self.ta[j]
        far = (a0 + 2) % 4
        w.wait(t[2], self.half(far, b, 0), down)
        w.wait(t[3], self.half(far, b, 1), up)
        self.have(far, b, 12 + j)

    def rest(self):
        self.along_b()
        self.along_a(0)
        self.along_b_far()
        self.along_a(3)
        self.along_a(1)
        self.along_a_far(0)
        self.along_a(2)
        for j in (3, 1, 2):
            self.along_a_far(j)


class Collect:
    def __init__(self, wire, piece, to, m, bufs):
        self.w, self.piece, self.m, self.bufs = wire, piece, m, bufs
        self.up, self.down = to((m + 1) % 4), to((m + 3) % 4)
        self.t = [wire.number() for _ in range(6)]

    def begin(self):
        out, inn = self.bufs
        m, w = self.m, self.w
        far = (m + 2) % 4
        out[0] = self.piece(far, 0).astype(out.dtype)
        w.start(self.t[0], out.at[0], inn.at[0], self.up)
        out[1] = self.piece(far, 1).astype(out.dtype)
        w.start(self.t[1], out.at[1], inn.at[1], self.down)
        out[2] = self.piece((m + 1) % 4, 1).astype(out.dtype)
        w.start(self.t[2], out.at[2], inn.at[2], self.up)
        out[3] = self.piece((m + 3) % 4, 0).astype(out.dtype)
        w.start(self.t[3], out.at[3], inn.at[3], self.down)

    def middle(self):
        out, inn = self.bufs
        m, w = self.m, self.w
        w.wait(self.t[0], inn.at[0], self.down)
        out[4] = (self.piece((m + 1) % 4, 0) + inn[0].astype(F32)).astype(out.dtype)
        w.start(self.t[4], out.at[4], inn.at[4], self.up)
        w.wait(self.t[1], inn.at[1], self.up)
        out[5] = (self.piece((m + 3) % 4, 1) + inn[1].astype(F32)).astype(out.dtype)
        w.start(self.t[5], out.at[5], inn.at[5], self.down)

    def end(self):
        out, inn = self.bufs
        m, w = self.m, self.w
        w.wait(self.t[2], inn.at[2], self.down)
        w.wait(self.t[3], inn.at[3], self.up)
        w.wait(self.t[4], inn.at[4], self.down)
        w.wait(self.t[5], inn.at[5], self.up)
        first = self.piece(m, 0) + (inn[4].astype(F32) + inn[3].astype(F32))
        second = self.piece(m, 1) + (inn[2].astype(F32) + inn[5].astype(F32))
        return first, second


def gather_kernel(entity_ref, table_ref, send, recv, local_sem):
    x, y, zh, zl, core = place()
    z_sign = 2 * zl - 1
    mine = pl.ds(pl.multiple_of(core * COLS, COLS), COLS)
    greet(x, y, zh, zl, core)
    w = Wire(send, recv)
    a0 = x * (1 - core) + y * core
    b0 = y * (1 - core) + x * core

    def block(a, b):
        return table_ref.at[a * (1 - core) + b * core, b * (1 - core) + a * core, :, mine]

    def to(a, b):
        return device(a * (1 - core) + b * core, b * (1 - core) + a * core, zh, zl, core)

    partner = device(x, y, zh, zl, 1 - core)
    tp = [w.number() for _ in range(16)]
    tz = [w.number() for _ in range(3)]

    def have(a, b, j):
        w.start(tp[j], block(a, b), block(a, b), partner)

    def rows(k):
        return block(a0, b0).at[pl.ds(pl.multiple_of(k * 16, 16), 16)]

    own = pltpu.make_async_copy(entity_ref.at[:, mine], rows(zh), local_sem)
    own.start()
    z_to = [((zh + z_sign + 4) % 4, 1 - zl), ((zh + z_sign + 4) % 4, zl), ((zh + 2) % 4, 1 - zl)]
    for t, (h, l) in zip(tz, z_to):
        w.start(t, entity_ref.at[:, mine], rows(zh), device(x, y, h, l, core))
    z_from = [(zh + z_sign + 4) % 4, (zh - z_sign + 4) % 4, (zh + 2) % 4]
    for t, h in zip(tz, z_from):
        w.wait(t, rows(h), partner)
    own.wait()
    spread = Spread(w, block, to, a0, b0, have)
    spread.begin()
    spread.rest()
    other = 1 - core
    theirs = pl.ds(pl.multiple_of(other * COLS, COLS), COLS)
    for j in range(16):
        w.wait(tp[j], table_ref.at[0, 0, :, theirs], partner)
    w.drain()


def gather_table(entity_table):
    messages = 16 + 3 + 20
    table = pl.pallas_call(
        gather_kernel,
        out_shape=jax.ShapeDtypeStruct((4, 4, 64, 2 * COLS), BF16),
        in_specs=[pl.BlockSpec(memory_space=VMEM)],
        out_specs=pl.BlockSpec(memory_space=VMEM),
        scratch_shapes=[
            pltpu.SemaphoreType.DMA((messages,)),
            pltpu.SemaphoreType.DMA((messages,)),
            pltpu.SemaphoreType.DMA,
        ],
        compiler_params=pltpu.CompilerParams(collective_id=0, has_side_effects=True),
        name="gather_table",
    )(entity_table)
    return table.reshape(1024, 1024)


def reduce_kernel(g_ref, d_ref, e_ref, r_ref, send, recv, pair, g_acc, g_out, g_in, h_out, h_in, g_small, z_in,
                  g_last, g_swap, d_out, d_in, f_out, f_in, d_small, d_zin):
    x, y, zh, zl, core = place()
    z = zh * 2 + zl
    other = 1 - core
    greet(x, y, zh, zl, core)
    w = Wire(send, recv)
    partner = device(x, y, zh, zl, other)
    ga, gb = x * other + y * core, y * other + x * core
    da, db = gb, ga

    def gxy(a, b):
        return a * other + b * core, b * other + a * core

    def dxy(a, b):
        return b * other + a * core, a * other + b * core

    def gto(a, b):
        px, py = gxy(a, b)
        return device(px, py, zh, zl, core)

    def dto(a, b):
        px, py = dxy(a, b)
        return device(px, py, zh, zl, core)

    tp = {}
    order = [(i, j) for i in (2, 1, 3, 0) for j in range(4)]
    for i, j in order:
        tp[i, j] = w.number()

    def pair_xy(a, b):
        return dxy(a, b)

    for i, j in order:
        px, py = pair_xy((gb + i) % 4, j)
        w.start(tp[i, j], g_ref.at[other, px, py], pair.at[px, py], partner)

    def d_piece(c, h):
        parts = []
        for b in (2 * h, 2 * h + 1):
            px, py = dxy(c, b)
            parts.append(d_ref[px, py][None])
        return jnp.concatenate(parts, axis=0)

    d_first = Collect(w, d_piece, lambda a: dto(a, db), da, (d_out, d_in))
    d_first.begin()

    for i, j in order:
        px, py = gxy((ga + i) % 4, j)
        w.wait(tp[i, j], pair.at[px, py], partner)
        g_acc[i, j] = g_ref[core, px, py] + pair[px, py]

    def g_piece(c, h):
        i = (c - ga + 4) % 4
        return g_acc[i, pl.ds(2 * h, 2)]

    g_first = Collect(w, g_piece, lambda a: gto(a, gb), ga, (g_out, g_in))
    g_first.begin()
    d_first.middle()
    g_first.middle()

    first, second = d_first.end()
    d_small[0:2] = first
    d_small[2:4] = second

    def d_piece2(c, h):
        return d_small[c, 32 * h:32 * h + 32]

    d_second = Collect(w, d_piece2, lambda b: dto(da, b), db, (f_out, f_in))
    d_second.begin()

    first, second = g_first.end()
    g_small[0:2] = first
    g_small[2:4] = second

    def g_piece2(c, h):
        return g_small[c, 32 * h:32 * h + 32]

    g_second = Collect(w, g_piece2, lambda b: gto(ga, b), gb, (h_out, h_in))
    g_second.begin()
    d_second.middle()
    g_second.middle()

    first, second = d_second.end()
    d_small[0, 0:32] = first
    d_small[0, 32:64] = second
    tdz = [w.number() for _ in range(3)]
    for k in range(1, 4):
        hh = (zh + k) % 4
        src = d_small.at[0, pl.ds(pl.multiple_of(hh * 16, 16), 16)]
        w.start(tdz[k - 1], src, d_zin.at[k - 1], device(x, y, hh, zl, core))

    first, second = g_second.end()
    g_small[0, 0:32] = first
    g_small[0, 32:64] = second
    tgz = [w.number() for _ in range(7)]
    for k in range(1, 8):
        zz = (z + k) % 8
        src = g_small.at[0, pl.ds(pl.multiple_of(zz * 8, 8), 8)]
        w.start(tgz[k - 1], src, z_in.at[k - 1], device(x, y, zz // 2, zz % 2, core))

    def block(a, b):
        px, py = dxy(a, b)
        return r_ref.at[px, py]

    total = d_small[0, pl.ds(pl.multiple_of(zh * 16, 16), 16)]
    for k in range(1, 4):
        w.wait(tdz[k - 1], d_zin.at[k - 1], partner)
    total = total + ((d_zin[0] + d_zin[1]) + d_zin[2])

    def rows(k):
        return block(da, db).at[pl.ds(pl.multiple_of(k * 16, 16), 16)]

    rows(zh)[...] = total.astype(r_ref.dtype)
    trz = [w.number() for _ in range(3)]
    for k in range(1, 4):
        w.start(trz[k - 1], rows(zh), rows(zh), device(x, y, (zh + k) % 4, zl, core))

    total = g_small[0, pl.ds(pl.multiple_of(z * 8, 8), 8)]
    for k in range(1, 8):
        w.wait(tgz[k - 1], z_in.at[k - 1], partner)
    for k in range(7):
        total = total + z_in[k]
    g_last[...] = total
    ts = w.number()
    w.start(ts, g_last, g_swap, partner)

    for k in range(1, 4):
        w.wait(trz[k - 1], rows((zh + 4 - k) % 4), partner)
    spread = Spread(w, block, dto, da, db, lambda a, b, j: None)
    spread.begin()

    w.wait(ts, g_swap, partner)
    here, there = g_last[...], g_swap[...]
    left = jnp.where(core == 0, here, there)
    right = jnp.where(core == 0, there, here)
    e_ref[:, 0:COLS] = jnp.where(core == 0, left[0:4], left[4:8])
    e_ref[:, COLS:2 * COLS] = jnp.where(core == 0, right[0:4], right[4:8])
    spread.rest()
    w.drain()


def reduce_all(g, d):
    messages = 16 + 6 * 4 + 3 + 7 + 3 + 1 + 20
    e, r = pl.pallas_call(
        reduce_kernel,
        out_shape=(jax.ShapeDtypeStruct((4, 2 * COLS), F32), jax.ShapeDtypeStruct((4, 4, 64, COLS), WIRE)),
        in_specs=[pl.BlockSpec(memory_space=VMEM)] * 2,
        out_specs=[pl.BlockSpec(memory_space=VMEM)] * 2,
        scratch_shapes=[
            pltpu.SemaphoreType.DMA((messages,)),
            pltpu.SemaphoreType.DMA((messages,)),
            VMEM((4, 4, 64, COLS), F32),
            VMEM((4, 4, 64, COLS), F32),
            VMEM((6, 2, 64, COLS), WIRE),
            VMEM((6, 2, 64, COLS), WIRE),
            VMEM((6, 32, COLS), WIRE),
            VMEM((6, 32, COLS), WIRE),
            VMEM((4, 64, COLS), F32),
            VMEM((7, 8, COLS), F32),
            VMEM((8, COLS), F32),
            VMEM((8, COLS), F32),
            VMEM((6, 2, 64, COLS), WIRE),
            VMEM((6, 2, 64, COLS), WIRE),
            VMEM((6, 32, COLS), WIRE),
            VMEM((6, 32, COLS), WIRE),
            VMEM((4, 64, COLS), F32),
            VMEM((3, 16, COLS), F32),
        ],
        compiler_params=pltpu.CompilerParams(collective_id=1, has_side_effects=True, vmem_limit_bytes=48 << 20),
        name="reduce_all",
    )(g.reshape(2, 4, 4, 64, COLS), d.reshape(4, 4, 64, COLS))
    return e, r.astype(F32).reshape(1024, COLS)


def compute_kernel(cols_ref, rows_ref, phases_ref, table_ref, g_ref, d_ref,
                   parts, cos_ref, sin_ref, word_ref, query_ref, weight_ref, back_ref, turn_ref, square_ref):
    rows_n, listed_n = 512, 32
    lanes = lax.broadcasted_iota(jnp.int32, (1, 1024), 1)
    lane = lax.broadcasted_iota(jnp.int32, (1, 128), 1)
    step = 128

    def dot(a, b):
        return jnp.dot(a, b, preferred_element_type=F32)

    def dot_nt(a, b):
        return lax.dot_general(a, b, (((1,), (1,)), ((), ())), preferred_element_type=F32)

    def dot_tn(a, b):
        return lax.dot_general(a, b, (((0,), (0,)), ((), ())), preferred_element_type=F32)

    def split(i, _):
        at = pl.ds(pl.multiple_of(i * step, step), step)
        p = phases_ref[at]
        for k in range(3):
            q = p.astype(BF16)
            parts[k, at] = q
            p = p - q.astype(F32)
        t = table_ref[at].astype(F32)
        s = jnp.sum(t * t, axis=1, keepdims=True)
        square_ref[i] = jnp.transpose(jnp.broadcast_to(s, (step, 128)))[0:8]
        return 0

    lax.fori_loop(0, 8, split, 0)

    def prepare(i, _):
        at = pl.ds(pl.multiple_of(i * step, step), step)
        ids = cols_ref[at]
        hot = (ids[:, 1:2] == lanes).astype(F32).astype(BF16)
        angle = dot(hot, parts[0]) + dot(hot, parts[1]) + dot(hot, parts[2])
        t = angle * angle
        c = horner(COS, t)
        s = angle * horner(SIN, t)
        cos_ref[at] = c
        sin_ref[at] = s
        low = ids & 127
        bit = jnp.left_shift(jnp.int32(1), jnp.right_shift(ids, 7))
        word = jnp.zeros((step, 128), jnp.int32)
        for j in range(3, 3 + listed_n):
            word = word | jnp.where(low[:, j:j + 1] == lane, bit[:, j:j + 1], 0)
        keep = jnp.where(low[:, 2:3] == lane, bit[:, 2:3], 0)
        word_ref[at] = (word & ~keep) | jnp.left_shift(keep, 8)
        return 0

    lax.fori_loop(0, rows_n // step, prepare, 0)

    def main(i, _):
        at = pl.ds(pl.multiple_of(i * step, step), step)
        ids = cols_ref[at]
        hot = (ids[:, 0:1] == lanes).astype(F32).astype(BF16)
        head = dot(hot, table_ref[...])
        c, s = cos_ref[at], sin_ref[at]
        hr, hm = head[:, :512], head[:, 512:]
        qr = hr * c - hm * s
        qm = hr * s + hm * c
        query = jnp.concatenate([qr, qm], axis=1).astype(BF16)
        query_ref[at] = query
        rounded = query.astype(F32)
        query_sq = jnp.sum(rounded * rounded, axis=1, keepdims=True)
        cross = dot_nt(query, table_ref[...])
        word = word_ref[at]
        scores, hidden = [], []
        top = None
        for k in range(8):
            sc = 2.0 * cross[:, k * 128:(k + 1) * 128] - query_sq - square_ref[k, 0:1]
            hide = (word & (1 << k)) != 0
            scores.append(sc)
            hidden.append(hide)
            seen = jnp.where(hide, -jnp.inf, sc)
            top = seen if top is None else jnp.maximum(top, seen)
        top = jnp.max(top, axis=1, keepdims=True)
        raws = []
        for k in range(8):
            raws.append(jnp.where(hidden[k], 0.0, jnp.exp(scores[k] - top)))
        total = raws[0]
        for k in range(1, 8):
            total = total + raws[k]
        scale = 1.0 / jnp.sum(total, axis=1, keepdims=True)
        weights = []
        for k in range(8):
            hit = (word & (256 << k)) != 0
            wk = (raws[k] * scale - jnp.where(hit, 1.0, 0.0)).astype(BF16)
            weights.append(wk)
            weight_ref[k, at] = wk
        grad = 2.0 * dot(jnp.concatenate(weights, axis=1), table_ref[...])
        gr, gm = grad[:, :512], grad[:, 512:]
        back_ref[at] = jnp.concatenate([gr * c + gm * s, gm * c - gr * s], axis=1).astype(BF16)
        turn = qr * gm - qm * gr
        high = turn.astype(BF16)
        turn_ref[0, at] = high
        turn_ref[1, at] = (turn - high.astype(F32)).astype(BF16)
        return 0

    lax.fori_loop(0, rows_n // step, main, 0)

    ones = jnp.ones((rows_n, 128), BF16)

    def finish(i, _):
        at = pl.ds(pl.multiple_of(i * step, step), step)
        key = lax.broadcasted_iota(jnp.int32, (step, 1), 0) + i * step
        wk = weight_ref[i]
        cross = dot_tn(wk, query_ref[...])
        counts = dot_tn(wk, ones)
        hot = (rows_ref[0:1] == key).astype(F32).astype(BF16)
        back = dot(hot, back_ref[...])
        t = table_ref[at].astype(F32)
        many = jnp.concatenate([counts] * 8, axis=1)
        out = 2.0 * (cross - many * t) + back
        g_ref[0, at] = out[:, :512]
        g_ref[1, at] = out[:, 512:]
        hot = (rows_ref[1:2] == key).astype(F32).astype(BF16)
        d_ref[at] = dot(hot, turn_ref[0]) + dot(hot, turn_ref[1])
        return 0

    lax.fori_loop(0, 8, finish, 0)


def compute(cols, rows, phases, table):
    return pl.pallas_call(
        compute_kernel,
        out_shape=(jax.ShapeDtypeStruct((2, 1024, COLS), F32), jax.ShapeDtypeStruct((1024, COLS), F32)),
        in_specs=[pl.BlockSpec(memory_space=VMEM)] * 4,
        out_specs=[pl.BlockSpec(memory_space=VMEM)] * 2,
        scratch_shapes=[
            VMEM((3, 1024, 512), BF16),
            VMEM((512, 512), F32),
            VMEM((512, 512), F32),
            VMEM((512, 128), jnp.int32),
            VMEM((512, 1024), BF16),
            VMEM((8, 512, 128), BF16),
            VMEM((512, 1024), BF16),
            VMEM((2, 512, 512), BF16),
            VMEM((8, 8, 128), F32),
        ],
        compiler_params=pltpu.CompilerParams(vmem_limit_bytes=56 << 20),
        name="compute",
    )(cols, rows, phases, table)


def local(entity_table, phases, head_owner, head_row, relation, tail_ids, known_tails):
    heads = head_owner[:, 0] * 4 + head_row
    cols = jnp.concatenate([heads[:, None], relation[:, None], tail_ids[:, None], known_tails], axis=1)
    rows = jnp.stack([heads, relation])
    table = gather_table(entity_table)
    g, d = compute(cols, rows, phases, table)
    return reduce_all(g, d)


def solution(mesh):
    in_specs = (
        P("ent", None),
        P("rel", None),
        P(("ent", "rel"), None),
        P(("ent", "rel")),
        P(("ent", "rel")),
        P(("ent", "rel")),
        P(("ent", "rel"), None),
    )
    out_specs = (P(("ent", "rel"), None), P("rel", None))
    return jax.shard_map(local, mesh=mesh, in_specs=in_specs, out_specs=out_specs, check_vma=False)
```

```python
import functools

import jax
import jax.numpy as jnp
from jax import lax
from jax.experimental import pallas as pl
from jax.experimental.pallas import tpu as pltpu
from jax.sharding import PartitionSpec as P

MESH = pl.DeviceIdType.MESH
VMEM = pltpu.VMEM
F32 = jnp.float32
BF16 = jnp.bfloat16
WIRE = jnp.bfloat16
COLS = 512

SIN = (0.9999999999932018, -0.16666666657817392, 0.008333333144447052, -0.00019841254471923497,
       2.7556704311932283e-06, -2.5038717712098566e-08, 1.5896746642760318e-10, -6.610935072102146e-13)
COS = (0.9999999999990714, -0.4999999999846839, 0.041666666625163704, -0.0013888888455803566,
       2.480156464708791e-05, -2.755665269895137e-07, 2.0865211281170485e-09, -1.1353643820753535e-11,
       4.131574377242709e-14)


def horner(coefficients, t):
    value = jnp.full_like(t, coefficients[-1])
    for c in coefficients[-2::-1]:
        value = value * t + c
    return value


def place():
    e = lax.axis_index("ent")
    r = lax.axis_index("rel")
    return e // 16, (e // 4) % 4, e % 4, r // 2, r % 2


def device(x, y, zh, zl, core):
    return {"ent": x * 16 + y * 4 + zh, "rel": zl * 2 + core}


class Wire:
    def __init__(self, send, recv):
        self.send, self.recv = send, recv
        self.count = 0
        self.open = []

    def number(self):
        self.count += 1
        return self.count - 1

    def start(self, t, src, dst, to):
        copy = pltpu.make_async_remote_copy(
            src_ref=src, dst_ref=dst, send_sem=self.send.at[t], recv_sem=self.recv.at[t],
            device_id=to, device_id_type=MESH)
        copy.start()
        self.open.append(copy)

    def wait(self, t, dst, to):
        pltpu.make_async_remote_copy(
            src_ref=dst, dst_ref=dst, send_sem=self.send.at[t], recv_sem=self.recv.at[t],
            device_id=to, device_id_type=MESH).wait_recv()

    def drain(self):
        for copy in self.open:
            copy.wait_send()
        self.open = []


def greet(x, y, zh, zl, core):
    barrier = pltpu.get_barrier_semaphore()
    z = zh * 2 + zl
    peers = [device(x, y, zh, zl, 1 - core)]
    for d in (1, 2, 3):
        peers.append(device((x + d) % 4, y, zh, zl, core))
        peers.append(device(x, (y + d) % 4, zh, zl, core))
    for d in range(1, 8):
        zz = (z + d) % 8
        peers.append(device(x, y, zz // 2, zz % 2, core))
    for peer in peers:
        pl.semaphore_signal(barrier, inc=1, device_id=peer, device_id_type=MESH)
    pl.semaphore_wait(barrier, len(peers))


class Spread:
    def __init__(self, wire, block, to, a0, b0, have):
        self.w, self.block, self.to, self.a0, self.b0, self.have = wire, block, to, a0, b0, have
        self.tb = [wire.number() for _ in range(3)]
        self.ta = [[wire.number() for _ in range(3)] for _ in range(4)]

    def got(self, j):
        b = (self.b0 + j) % 4
        blk = self.block(self.a0, b)
        for k in (2, 1, 3):
            self.w.start(self.ta[j][k - 1], blk, blk, self.to((self.a0 + k) % 4, self.b0))
        self.have(self.a0, b, j)

    def begin(self):
        blk = self.block(self.a0, self.b0)
        for k in (2, 1, 3):
            self.w.start(self.tb[k - 1], blk, blk, self.to(self.a0, (self.b0 + k) % 4))
        self.got(0)

    def along_b(self):
        for k in (1, 3, 2):
            j = 4 - k
            b = (self.b0 + j) % 4
            self.w.wait(self.tb[k - 1], self.block(self.a0, b), self.to(self.a0, b))
            self.got(j)

    def along_a(self, j):
        b = (self.b0 + j) % 4
        for k in (1, 3, 2):
            a = (self.a0 + 4 - k) % 4
            self.w.wait(self.ta[j][k - 1], self.block(a, b), self.to(a, self.b0))
            self.have(a, b, 4 * k + j)


class Collect:
    def __init__(self, wire, piece, to, m, out, inn):
        self.w, self.piece, self.to, self.m, self.out, self.inn = wire, piece, to, m, out, inn
        self.t = [wire.number() for _ in range(3)]

    def begin(self):
        for k in (2, 1, 3):
            c = (self.m + k) % 4
            self.out[k - 1] = self.piece(c).astype(self.out.dtype)
            self.w.start(self.t[k - 1], self.out.at[k - 1], self.inn.at[k - 1], self.to(c))

    def end(self):
        for k in (1, 3, 2):
            self.w.wait(self.t[k - 1], self.inn.at[k - 1], self.to((self.m + 4 - k) % 4))
        inn = self.inn
        return self.piece(self.m) + ((inn[0].astype(F32) + inn[2].astype(F32)) + inn[1].astype(F32))


def dot(a, b):
    return jnp.dot(a, b, preferred_element_type=F32)


def dot_nt(a, b):
    return lax.dot_general(a, b, (((1,), (1,)), ((), ())), preferred_element_type=F32)


def dot_tn(a, b):
    return lax.dot_general(a, b, (((0,), (0,)), ((), ())), preferred_element_type=F32)


def span(i, n):
    return pl.ds(pl.multiple_of(i * n, n), n)


STEP = 128
TRIPLES = 512
LISTED = 32


def step_kernel(known_ref, owner_ref, place_ref, relation_ref, tail_ref, phases_hbm, entity_ref, e_ref, r_ref,
                send, recv, local_sem, phases_sem,
                phases_ref, parts, cos_ref, sin_ref, word_ref, head_ref, table_ref, square_ref,
                query_ref, weight_ref, back_ref, turn_ref, g_ref, pair, d_ref,
                g_acc, g_out, g_in, h_out, h_in, g_small, z_in, g_last, g_swap,
                d_out, d_in, f_out, f_in, d_small, d_zin):
    x, y, zh, zl, core = place()
    z = zh * 2 + zl
    other = 1 - core
    z_sign = 2 * zl - 1
    mine = span(core, COLS)
    theirs = span(other, COLS)
    partner = device(x, y, zh, zl, other)
    w = Wire(send, recv)

    fetch = pltpu.make_async_copy(phases_hbm, phases_ref, phases_sem)
    fetch.start()
    ga, gb = x * other + y * core, y * other + x * core
    da, db = gb, ga

    def gxy(a, b):
        return a * other + b * core, b * other + a * core

    def dxy(a, b):
        return b * other + a * core, a * other + b * core

    def gspan(a, b):
        px, py = gxy(a, b)
        return span(px * 4 + py, 64)

    def dspan(a, b):
        px, py = dxy(a, b)
        return span(px * 4 + py, 64)

    def gto(a, b):
        px, py = gxy(a, b)
        return device(px, py, zh, zl, core)

    def dto(a, b):
        px, py = dxy(a, b)
        return device(px, py, zh, zl, core)

    greet(x, y, zh, zl, core)

    tp = [w.number() for _ in range(16)]
    tz = [w.number() for _ in range(3)]

    def block(a, b):
        return table_ref.at[gspan(a, b), mine]

    def rows(k):
        return table_ref.at[pl.ds(pl.multiple_of((x * 4 + y) * 64 + k * 16, 16), 16), mine]

    own = pltpu.make_async_copy(entity_ref.at[:, mine], rows(zh), local_sem)
    own.start()
    z_to = [((zh + z_sign + 4) % 4, 1 - zl), ((zh + z_sign + 4) % 4, zl), ((zh + 2) % 4, 1 - zl)]
    for t, (h, l) in zip(tz, z_to):
        w.start(t, entity_ref.at[:, mine], rows(zh), device(x, y, h, l, core))

    fetch.wait()

    def split(i, _):
        at = span(i, STEP)
        p = phases_ref[at]
        for k in range(3):
            q = p.astype(BF16)
            parts[k, at] = q
            p = p - q.astype(F32)
        return 0

    lax.fori_loop(0, 8, split, 0)

    lane = lax.broadcasted_iota(jnp.int32, (1, STEP), 1)

    def down(row):
        return jnp.transpose(jnp.broadcast_to(row, (STEP, STEP)))

    def hot_rows(col):
        return jnp.concatenate([(col == lane + 128 * k).astype(F32).astype(BF16) for k in range(8)], axis=1)

    def prepare(i, _):
        at = span(i, STEP)
        head_ref[at] = down(owner_ref[:, at] * 4 + place_ref[:, at])
        hot = hot_rows(down(relation_ref[:, at]))
        angle = dot(hot, parts[0]) + dot(hot, parts[1]) + dot(hot, parts[2])
        t = angle * angle
        cos_ref[at] = horner(COS, t)
        sin_ref[at] = angle * horner(SIN, t)
        ids = jnp.transpose(known_ref[:, at])
        low = ids & 127
        bit = jnp.left_shift(jnp.int32(1), jnp.right_shift(ids, 7))
        word = jnp.zeros((STEP, STEP), jnp.int32)
        for j in range(LISTED):
            word = word | jnp.where(low[:, j:j + 1] == lane, bit[:, j:j + 1], 0)
        tail = down(tail_ref[:, at])
        keep = jnp.where((tail & 127) == lane, jnp.left_shift(jnp.int32(1), jnp.right_shift(tail, 7)), 0)
        word_ref[at] = (word & ~keep) | jnp.left_shift(keep, 8)
        return 0

    lax.fori_loop(0, 1, prepare, 0)
    z_from = [(zh + z_sign + 4) % 4, (zh - z_sign + 4) % 4, (zh + 2) % 4]
    for t, h in zip(tz, z_from):
        w.wait(t, rows(h), partner)
    own.wait()

    def have(a, b, j):
        w.start(tp[j], block(a, b), block(a, b), partner)

    spread = Spread(w, block, gto, ga, gb, have)
    spread.begin()
    lax.fori_loop(1, 2, prepare, 0)
    spread.along_b()
    lax.fori_loop(2, 4, prepare, 0)
    for j in (0, 3, 1, 2):
        spread.along_a(j)
    for j in range(16):
        w.wait(tp[j], table_ref.at[pl.ds(0, 64), theirs], partner)

    def squares(i, _):
        t = table_ref[span(i, STEP)].astype(F32)
        s = jnp.sum(t * t, axis=1, keepdims=True)
        square_ref[i] = jnp.transpose(jnp.broadcast_to(s, (STEP, STEP)))[0:8]
        return 0

    lax.fori_loop(0, 8, squares, 0)

    def main(i, _):
        at = span(i, STEP)
        head = dot(hot_rows(head_ref[at]), table_ref[...])
        c, s = cos_ref[at], sin_ref[at]
        hr, hm = head[:, :COLS], head[:, COLS:]
        qr = hr * c - hm * s
        qm = hr * s + hm * c
        query = jnp.concatenate([qr, qm], axis=1).astype(BF16)
        query_ref[at] = query
        rounded = query.astype(F32)
        query_sq = jnp.sum(rounded * rounded, axis=1, keepdims=True)
        cross = dot_nt(query, table_ref[...])
        word = word_ref[at]
        scores, hidden = [], []
        top = None
        for k in range(8):
            sc = 2.0 * cross[:, k * 128:(k + 1) * 128] - query_sq - square_ref[k, 0:1]
            hide = (word & (1 << k)) != 0
            scores.append(sc)
            hidden.append(hide)
            seen = jnp.where(hide, -jnp.inf, sc)
            top = seen if top is None else jnp.maximum(top, seen)
        top = jnp.max(top, axis=1, keepdims=True)
        raws = []
        for k in range(8):
            raws.append(jnp.where(hidden[k], 0.0, jnp.exp(scores[k] - top)))
        total = raws[0]
        for k in range(1, 8):
            total = total + raws[k]
        scale = 1.0 / jnp.sum(total, axis=1, keepdims=True)
        weights = []
        for k in range(8):
            hit = (word & (256 << k)) != 0
            wk = (raws[k] * scale - jnp.where(hit, 1.0, 0.0)).astype(BF16)
            weights.append(wk)
            weight_ref[k, at] = wk
        grad = 2.0 * dot(jnp.concatenate(weights, axis=1), table_ref[...])
        gr, gm = grad[:, :COLS], grad[:, COLS:]
        back_ref[at] = jnp.concatenate([gr * c + gm * s, gm * c - gr * s], axis=1).astype(BF16)
        turn = qr * gm - qm * gr
        high = turn.astype(BF16)
        turn_ref[0, at] = high
        turn_ref[1, at] = (turn - high.astype(F32)).astype(BF16)
        return 0

    lax.fori_loop(0, TRIPLES // STEP, main, 0)

    def key(i):
        return lax.broadcasted_iota(jnp.int32, (STEP, 1), 0) + i * STEP

    def relations(i, _):
        hot = (relation_ref[...] == key(i)).astype(F32).astype(BF16)
        d_ref[span(i, STEP)] = dot(hot, turn_ref[0]) + dot(hot, turn_ref[1])
        return 0

    lax.fori_loop(0, 8, relations, 0)

    def d_piece(c):
        return jnp.concatenate([d_ref[dspan(c, b)][None] for b in range(4)], axis=0)

    d_first = Collect(w, d_piece, lambda a: dto(a, db), da, d_out, d_in)
    d_first.begin()

    ones = jnp.ones((TRIPLES, 128), BF16)
    heads = owner_ref[...] * 4 + place_ref[...]

    def dense(i):
        at = span(i, STEP)
        wk = weight_ref[i]
        cross = dot_tn(wk, query_ref[...])
        counts = dot_tn(wk, ones)
        hot = (heads == key(i)).astype(F32).astype(BF16)
        back = dot(hot, back_ref[...])
        t = table_ref[at].astype(F32)
        many = jnp.concatenate([counts] * 8, axis=1)
        out = 2.0 * (cross - many * t) + back
        g_ref[0, at] = out[:, :COLS]
        g_ref[1, at] = out[:, COLS:]

    tg = [w.number() for _ in range(8)]

    def turn_of(n):
        return (x * 2 + 4 + n) % 8

    for n in range(8):
        i = turn_of(n)
        dense(i)
        w.start(tg[n], g_ref.at[other, span(i, STEP)], pair.at[span(i, STEP)], partner)

    def add_pair(n):
        i = turn_of(n)
        w.wait(tg[n], pair.at[span(i, STEP)], partner)
        g_acc[span(i, STEP)] = g_ref[core, span(i, STEP)] + pair[span(i, STEP)]

    for n in range(8):
        add_pair(n)

    def g_piece(c):
        return jnp.concatenate([g_acc[gspan(c, b)][None] for b in range(4)], axis=0)

    g_first = Collect(w, g_piece, lambda a: gto(a, gb), ga, g_out, g_in)
    g_first.begin()

    d_small[...] = d_first.end()
    d_second = Collect(w, lambda c: d_small[c], lambda b: dto(da, b), db, f_out, f_in)
    d_second.begin()

    tdz = [w.number() for _ in range(3)]
    tgz = [w.number() for _ in range(7)]
    trz = [w.number() for _ in range(3)]
    ts = w.number()
    d_small[0] = d_second.end()
    for k in (2, 1, 3):
        hh = (zh + k) % 4
        w.start(tdz[k - 1], d_small.at[0, span(hh, 16)], d_zin.at[k - 1], device(x, y, hh, zl, core))

    g_small[...] = g_first.end()
    g_second = Collect(w, lambda c: g_small[c], lambda b: gto(ga, b), gb, h_out, h_in)
    g_second.begin()

    def r_block(a, b):
        return r_ref.at[dspan(a, b)]

    def r_rows(k):
        return r_ref.at[pl.ds(pl.multiple_of((x * 4 + y) * 64 + k * 16, 16), 16)]

    for k in (1, 3, 2):
        w.wait(tdz[k - 1], d_zin.at[k - 1], partner)
    total = d_small[0, span(zh, 16)] + ((d_zin[0] + d_zin[1]) + d_zin[2])
    r_rows(zh)[...] = total.astype(r_ref.dtype)
    for k in (2, 1, 3):
        w.start(trz[k - 1], r_rows(zh), r_rows(zh), device(x, y, (zh + k) % 4, zl, core))

    g_small[0] = g_second.end()
    for k in (4, 3, 5, 2, 6, 1, 7):
        zz = (z + k) % 8
        w.start(tgz[k - 1], g_small.at[0, span(zz, 8)], z_in.at[k - 1], device(x, y, zz // 2, zz % 2, core))

    for k in (1, 3, 2):
        w.wait(trz[k - 1], r_rows((zh + 4 - k) % 4), partner)
    back = Spread(w, r_block, dto, da, db, lambda a, b, j: None)
    back.begin()

    total = g_small[0, span(z, 8)]
    for k in range(1, 8):
        w.wait(tgz[k - 1], z_in.at[k - 1], partner)
    for k in range(7):
        total = total + z_in[k]
    g_last[...] = total
    w.start(ts, g_last, g_swap, partner)

    back.along_b()
    w.wait(ts, g_swap, partner)
    here, there = g_last[...], g_swap[...]
    left = jnp.where(core == 0, here, there)
    right = jnp.where(core == 0, there, here)
    e_ref[:, 0:COLS] = jnp.where(core == 0, left[0:4], left[4:8])
    e_ref[:, COLS:2 * COLS] = jnp.where(core == 0, right[0:4], right[4:8])
    for j in (0, 3, 1, 2):
        back.along_a(j)
    w.drain()


def local(entity_table, phases, head_owner, head_row, relation, tail_ids, known_tails):
    messages = 16 + 3 + 15 + 12 + 8 + 3 + 7 + 3 + 1 + 15
    here = pl.BlockSpec(memory_space=VMEM)
    e, r = pl.pallas_call(
        step_kernel,
        out_shape=(jax.ShapeDtypeStruct((4, 2 * COLS), F32), jax.ShapeDtypeStruct((1024, COLS), WIRE)),
        in_specs=[here] * 5 + [pl.BlockSpec(memory_space=pl.ANY), here],
        out_specs=[here, here],
        scratch_shapes=[
            pltpu.SemaphoreType.DMA((messages,)),
            pltpu.SemaphoreType.DMA((messages,)),
            pltpu.SemaphoreType.DMA,
            pltpu.SemaphoreType.DMA,
            VMEM((1024, COLS), F32),
            VMEM((3, 1024, COLS), BF16),
            VMEM((TRIPLES, COLS), F32),
            VMEM((TRIPLES, COLS), F32),
            VMEM((TRIPLES, STEP), jnp.int32),
            VMEM((TRIPLES, STEP), jnp.int32),
            VMEM((1024, 2 * COLS), BF16),
            VMEM((8, 8, STEP), F32),
            VMEM((TRIPLES, 2 * COLS), BF16),
            VMEM((8, TRIPLES, STEP), BF16),
            VMEM((TRIPLES, 2 * COLS), BF16),
            VMEM((2, TRIPLES, COLS), BF16),
            VMEM((2, 1024, COLS), F32),
            VMEM((1024, COLS), F32),
            VMEM((1024, COLS), F32),
            VMEM((1024, COLS), F32),
            VMEM((3, 4, 64, COLS), WIRE),
            VMEM((3, 4, 64, COLS), WIRE),
            VMEM((3, 64, COLS), WIRE),
            VMEM((3, 64, COLS), WIRE),
            VMEM((4, 64, COLS), F32),
            VMEM((7, 8, COLS), F32),
            VMEM((8, COLS), F32),
            VMEM((8, COLS), F32),
            VMEM((3, 4, 64, COLS), WIRE),
            VMEM((3, 4, 64, COLS), WIRE),
            VMEM((3, 64, COLS), WIRE),
            VMEM((3, 64, COLS), WIRE),
            VMEM((4, 64, COLS), F32),
            VMEM((3, 16, COLS), F32),
        ],
        compiler_params=pltpu.CompilerParams(collective_id=0, has_side_effects=True, vmem_limit_bytes=58 << 20),
        name="step",
    )(known_tails.T, head_owner.reshape(1, TRIPLES), head_row.reshape(1, TRIPLES), relation.reshape(1, TRIPLES),
      tail_ids.reshape(1, TRIPLES), phases, entity_table)
    return e, r.astype(F32)


def solution(mesh):
    in_specs = (
        P("ent", None),
        P("rel", None),
        P(("ent", "rel"), None),
        P(("ent", "rel")),
        P(("ent", "rel")),
        P(("ent", "rel")),
        P(("ent", "rel"), None),
    )
    out_specs = (P(("ent", "rel"), None), P("rel", None))
    return jax.shard_map(local, mesh=mesh, in_specs=in_specs, out_specs=out_specs, check_vma=False)
```

```python
import functools

import jax
import jax.numpy as jnp
from jax import lax
from jax.experimental import pallas as pl
from jax.experimental.pallas import tpu as pltpu
from jax.sharding import PartitionSpec as P

MESH = pl.DeviceIdType.MESH
VMEM = pltpu.VMEM
F32 = jnp.float32
BF16 = jnp.bfloat16
WIRE = jnp.bfloat16
COLS = 512

SIN = (0.9999999999932018, -0.16666666657817392, 0.008333333144447052, -0.00019841254471923497,
       2.7556704311932283e-06, -2.5038717712098566e-08, 1.5896746642760318e-10, -6.610935072102146e-13)
COS = (0.9999999999990714, -0.4999999999846839, 0.041666666625163704, -0.0013888888455803566,
       2.480156464708791e-05, -2.755665269895137e-07, 2.0865211281170485e-09, -1.1353643820753535e-11,
       4.131574377242709e-14)


def horner(coefficients, t):
    value = jnp.full_like(t, coefficients[-1])
    for c in coefficients[-2::-1]:
        value = value * t + c
    return value


def place():
    e = lax.axis_index("ent")
    r = lax.axis_index("rel")
    return e // 16, (e // 4) % 4, e % 4, r // 2, r % 2


def device(x, y, zh, zl, core):
    return {"ent": x * 16 + y * 4 + zh, "rel": zl * 2 + core}


class Wire:
    def __init__(self, send, recv):
        self.send, self.recv = send, recv
        self.count = 0
        self.open = []

    def number(self):
        self.count += 1
        return self.count - 1

    def start(self, t, src, dst, to):
        copy = pltpu.make_async_remote_copy(
            src_ref=src, dst_ref=dst, send_sem=self.send.at[t], recv_sem=self.recv.at[t],
            device_id=to, device_id_type=MESH)
        copy.start()
        self.open.append(copy)

    def wait(self, t, dst, to):
        pltpu.make_async_remote_copy(
            src_ref=dst, dst_ref=dst, send_sem=self.send.at[t], recv_sem=self.recv.at[t],
            device_id=to, device_id_type=MESH).wait_recv()

    def drain(self):
        for copy in self.open:
            copy.wait_send()
        self.open = []


def greet(x, y, zh, zl, core):
    barrier = pltpu.get_barrier_semaphore()
    z = zh * 2 + zl
    peers = [device(x, y, zh, zl, 1 - core)]
    for d in (1, 2, 3):
        peers.append(device((x + d) % 4, y, zh, zl, core))
        peers.append(device(x, (y + d) % 4, zh, zl, core))
    for d in range(1, 8):
        zz = (z + d) % 8
        peers.append(device(x, y, zz // 2, zz % 2, core))
    for peer in peers:
        pl.semaphore_signal(barrier, inc=1, device_id=peer, device_id_type=MESH)
    pl.semaphore_wait(barrier, len(peers))


class Spread:
    def __init__(self, wire, block, to, a0, b0, own, z_to, z_from):
        self.w, self.block, self.to, self.a0, self.b0 = wire, block, to, a0, b0
        self.z_to, self.ks = z_to, [own] + z_from
        self.tz = [wire.number() for _ in range(3)]
        self.tb = [[wire.number() for _ in range(3)] for _ in range(4)]
        self.ta = [[[wire.number() for _ in range(3)] for _ in range(4)] for _ in range(4)]

    def along(self, q, j):
        blk = self.block(self.a0, (self.b0 + j) % 4, self.ks[q])
        for k in (2, 1, 3):
            self.w.start(self.ta[q][j][k - 1], blk, blk, self.to((self.a0 + k) % 4, self.b0))

    def on(self, q):
        blk = self.block(self.a0, self.b0, self.ks[q])
        for k in (2, 1, 3):
            self.w.start(self.tb[q][k - 1], blk, blk, self.to(self.a0, (self.b0 + k) % 4))
        self.along(q, 0)

    def begin(self):
        blk = self.block(self.a0, self.b0, self.ks[0])
        for i in range(3):
            self.w.start(self.tz[i], blk, blk, self.z_to[i])
        self.on(0)

    def take_z(self, i):
        self.w.wait(self.tz[i], self.block(self.a0, self.b0, self.ks[1 + i]), self.z_to[i])
        self.on(1 + i)

    def take_b(self, q):
        for k in (1, 3, 2):
            j = 4 - k
            b = (self.b0 + j) % 4
            self.w.wait(self.tb[q][k - 1], self.block(self.a0, b, self.ks[q]), self.to(self.a0, b))
            self.along(q, j)

    def take_a(self, q, j):
        for k in (1, 3, 2):
            a = (self.a0 + 4 - k) % 4
            self.w.wait(self.ta[q][j][k - 1], self.block(a, (self.b0 + j) % 4, self.ks[q]), self.to(a, self.b0))


FAR = (2, 1, 3, 0)


class Chain:
    def __init__(self, wire, load, to, a0, b0, zh, bufs):
        self.w, self.load, self.to, self.a0, self.b0 = wire, load, to, a0, b0
        self.ks = [(zh + off) % 4 for off in FAR]
        self.out_a, self.in_a, self.small, self.out_b, self.in_b, self.last = bufs
        self.ta = [[wire.number() for _ in range(3)] for _ in range(4)]
        self.tb = [[wire.number() for _ in range(3)] for _ in range(4)]

    def piece(self, c, q):
        return jnp.concatenate([self.load(c, b, self.ks[q])[None] for b in range(4)], axis=0)

    def begin_a(self, q):
        for k in (2, 1, 3):
            c = (self.a0 + k) % 4
            self.out_a[k - 1, q] = self.piece(c, q).astype(self.out_a.dtype)
            self.w.start(self.ta[q][k - 1], self.out_a.at[k - 1, q], self.in_a.at[k - 1, q], self.to(c, self.b0))

    def turn_b(self, q):
        for k in (1, 3, 2):
            self.w.wait(self.ta[q][k - 1], self.in_a.at[k - 1, q], self.to((self.a0 + 4 - k) % 4, self.b0))
        near = self.in_a[0, q].astype(F32) + self.in_a[2, q].astype(F32)
        self.small[q] = self.piece(self.a0, q) + (near + self.in_a[1, q].astype(F32))
        for k in (2, 1, 3):
            c = (self.b0 + k) % 4
            self.out_b[k - 1, q] = self.small[q, c].astype(self.out_b.dtype)
            self.w.start(self.tb[q][k - 1], self.out_b.at[k - 1, q], self.in_b.at[k - 1, q], self.to(self.a0, c))

    def end_b(self, q):
        for k in (1, 3, 2):
            self.w.wait(self.tb[q][k - 1], self.in_b.at[k - 1, q], self.to(self.a0, (self.b0 + 4 - k) % 4))
        near = self.in_b[0, q].astype(F32) + self.in_b[2, q].astype(F32)
        self.last[q] = self.small[q, self.b0] + (near + self.in_b[1, q].astype(F32))


def dot(a, b):
    return jnp.dot(a, b, preferred_element_type=F32)


def dot_nt(a, b):
    return lax.dot_general(a, b, (((1,), (1,)), ((), ())), preferred_element_type=F32)


def dot_tn(a, b):
    return lax.dot_general(a, b, (((0,), (0,)), ((), ())), preferred_element_type=F32)


def span(i, n):
    return pl.ds(pl.multiple_of(i * n, n), n)


STEP = 128
MAIN = 256
DENSE = 256
TRIPLES = 512
LISTED = 32


def step_kernel(known_ref, owner_ref, place_ref, relation_ref, tail_ref, phases_hbm, entity_ref, e_ref, r_ref,
                send, recv, local_sem, phases_sem,
                phases_ref, parts, cos_ref, sin_ref, word_ref, head_ref, table_ref, square_ref,
                query_ref, weight_ref, back_ref, turn_ref, g_ref, pair, d_ref,
                ga_out, ga_in, g_small, gb_out, gb_in, g_sum, g_zin, g_last, g_swap,
                da_out, da_in, d_small, db_out, db_in, d_sum, d_zin):
    x, y, zh, zl, core = place()
    other = 1 - core
    z_sign = 2 * zl - 1
    mine = span(core, COLS)
    theirs = span(other, COLS)
    partner = device(x, y, zh, zl, other)
    w = Wire(send, recv)

    fetch = pltpu.make_async_copy(phases_hbm, phases_ref, phases_sem)
    fetch.start()
    ga, gb = x * other + y * core, y * other + x * core
    da, db = gb, ga

    def gxy(a, b):
        return a * other + b * core, b * other + a * core

    def dxy(a, b):
        return b * other + a * core, a * other + b * core

    def gspan(a, b):
        px, py = gxy(a, b)
        return span(px * 4 + py, 64)

    def dspan(a, b):
        px, py = dxy(a, b)
        return span(px * 4 + py, 64)

    def gto(a, b):
        px, py = gxy(a, b)
        return device(px, py, zh, zl, core)

    def dto(a, b):
        px, py = dxy(a, b)
        return device(px, py, zh, zl, core)

    greet(x, y, zh, zl, core)

    tp = [w.number() for _ in range(16)]

    def block(a, b, k):
        px, py = gxy(a, b)
        return table_ref.at[core, span((px * 4 + py) * 4 + k, 16)]

    z_to = [device(x, y, (zh + z_sign + 4) % 4, 1 - zl, core), device(x, y, (zh + z_sign + 4) % 4, zl, core),
            device(x, y, (zh + 2) % 4, 1 - zl, core)]
    z_from = [(zh + z_sign + 4) % 4, (zh - z_sign + 4) % 4, (zh + 2) % 4]
    own = pltpu.make_async_copy(entity_ref.at[:, mine], block(ga, gb, zh), local_sem)
    own.start()
    own.wait()
    spread = Spread(w, block, gto, ga, gb, zh, z_to, z_from)
    spread.begin()

    def push(i, a, b):
        part = table_ref.at[core, gspan(a, b)]
        w.start(tp[i], part, part, partner)

    fetch.wait()

    def split(i, _):
        at = span(i, STEP)
        p = phases_ref[at]
        for k in range(3):
            q = p.astype(BF16)
            parts[k, at] = q
            p = p - q.astype(F32)
        return 0

    lax.fori_loop(0, 8, split, 0)

    lane = lax.broadcasted_iota(jnp.int32, (1, STEP), 1)

    def down(row):
        return jnp.transpose(jnp.broadcast_to(row, (STEP, STEP)))

    def hot_rows(col):
        return jnp.concatenate([(col == lane + 128 * k).astype(F32).astype(BF16) for k in range(8)], axis=1)

    def prepare(i, _):
        at = span(i, STEP)
        head_ref[at] = down(owner_ref[:, at] * 4 + place_ref[:, at])
        hot = hot_rows(down(relation_ref[:, at]))
        angle = dot(hot, parts[0]) + dot(hot, parts[1]) + dot(hot, parts[2])
        t = angle * angle
        cos_ref[at] = horner(COS, t)
        sin_ref[at] = angle * horner(SIN, t)
        ids = jnp.transpose(known_ref[:, at])
        low = ids & 127
        bit = jnp.left_shift(jnp.int32(1), jnp.right_shift(ids, 7))
        word = jnp.zeros((STEP, STEP), jnp.int32)
        for j in range(LISTED):
            word = word | jnp.where(low[:, j:j + 1] == lane, bit[:, j:j + 1], 0)
        tail = down(tail_ref[:, at])
        keep = jnp.where((tail & 127) == lane, jnp.left_shift(jnp.int32(1), jnp.right_shift(tail, 7)), 0)
        word_ref[at] = (word & ~keep) | jnp.left_shift(keep, 8)
        return 0

    spread.take_z(0)
    spread.take_b(0)
    lax.fori_loop(0, 1, prepare, 0)
    spread.take_z(1)
    spread.take_z(2)
    lax.fori_loop(1, 2, prepare, 0)
    for q in (1, 2, 3):
        spread.take_b(q)
    for j in range(4):
        push(j, ga, (gb + j) % 4)
    lax.fori_loop(2, 4, prepare, 0)
    for j in (0, 3, 1, 2):
        for q in range(4):
            spread.take_a(q, j)
        for k in (1, 3, 2):
            push(4 * k + j, (ga + 4 - k) % 4, (gb + j) % 4)
    for i in range(16):
        w.wait(tp[i], table_ref.at[other, pl.ds(0, 64)], partner)

    def squares(i, _):
        re, im = table_ref[0, span(i, STEP)].astype(F32), table_ref[1, span(i, STEP)].astype(F32)
        s = jnp.sum(re * re + im * im, axis=1, keepdims=True)
        square_ref[i] = jnp.transpose(jnp.broadcast_to(s, (STEP, STEP)))[0:8]
        return 0

    lax.fori_loop(0, 8, squares, 0)

    def main(i, _):
        at = span(i, MAIN)
        hot = hot_rows(head_ref[at])
        c, s = cos_ref[at], sin_ref[at]
        hr, hm = dot(hot, table_ref[0]), dot(hot, table_ref[1])
        qr = hr * c - hm * s
        qm = hr * s + hm * c
        query_r, query_m = qr.astype(BF16), qm.astype(BF16)
        query_ref[0, at] = query_r
        query_ref[1, at] = query_m
        near_r, near_m = query_r.astype(F32), query_m.astype(F32)
        query_sq = jnp.sum(near_r * near_r + near_m * near_m, axis=1, keepdims=True)
        cross = dot_nt(query_r, table_ref[0]) + dot_nt(query_m, table_ref[1])
        word = word_ref[at]
        scores, hidden = [], []
        top = None
        for k in range(8):
            sc = 2.0 * cross[:, k * 128:(k + 1) * 128] - query_sq - square_ref[k, 0:1]
            hide = (word & (1 << k)) != 0
            scores.append(sc)
            hidden.append(hide)
            seen = jnp.where(hide, -jnp.inf, sc)
            top = seen if top is None else jnp.maximum(top, seen)
        top = jnp.max(top, axis=1, keepdims=True)
        raws = []
        for k in range(8):
            raws.append(jnp.where(hidden[k], 0.0, jnp.exp(scores[k] - top)))
        total = raws[0]
        for k in range(1, 8):
            total = total + raws[k]
        scale = 2.0 / jnp.sum(total, axis=1, keepdims=True)
        weights = []
        for k in range(8):
            hit = (word & (256 << k)) != 0
            wk = (raws[k] * scale - jnp.where(hit, 2.0, 0.0)).astype(BF16)
            weights.append(wk)
            weight_ref[k, at] = wk
        both = jnp.concatenate(weights, axis=1)
        gr, gm = dot(both, table_ref[0]), dot(both, table_ref[1])
        back_ref[0, at] = (gr * c + gm * s).astype(BF16)
        back_ref[1, at] = (gm * c - gr * s).astype(BF16)
        turn = qr * gm - qm * gr
        high = turn.astype(BF16)
        turn_ref[0, at] = high
        turn_ref[1, at] = (turn - high.astype(F32)).astype(BF16)
        return 0

    lax.fori_loop(0, TRIPLES // MAIN, main, 0)

    def key(i):
        return lax.broadcasted_iota(jnp.int32, (DENSE, 1), 0) + i * DENSE

    def relations(i, _):
        hot = (relation_ref[...] == key(i)).astype(F32).astype(BF16)
        d_ref[span(i, DENSE)] = dot(hot, turn_ref[0]) + dot(hot, turn_ref[1])
        return 0

    lax.fori_loop(0, 1024 // DENSE, relations, 0)

    def d_load(a, b, k):
        px, py = dxy(a, b)
        return d_ref[span((px * 4 + py) * 4 + k, 16)]

    d_chain = Chain(w, d_load, dto, da, db, zh, (da_out, da_in, d_small, db_out, db_in, d_sum))
    for q in range(4):
        d_chain.begin_a(q)

    ones = jnp.ones((TRIPLES, 128), BF16)
    heads = owner_ref[...] * 4 + place_ref[...]

    def dense(i):
        at = span(i, DENSE)
        wk = jnp.concatenate([weight_ref[i * (DENSE // 128) + k] for k in range(DENSE // 128)], axis=1)
        counts = dot_tn(wk, ones)
        hot = (heads == key(i)).astype(F32).astype(BF16)
        many = jnp.concatenate([counts] * 4, axis=1)
        for c in range(2):
            sums = dot_tn(wk, query_ref[c]) + dot(hot, back_ref[c])
            g_ref[c, at] = sums - many * table_ref[c, at].astype(F32)

    tg = [w.number() for _ in range(4)]

    def dense_of(n):
        i = (x + 2 + n) % 4
        dense(i)
        w.start(tg[n], g_ref.at[other, span(i, DENSE)], pair.at[span(i, DENSE)], partner)

    dense_of(0)
    dense_of(1)
    d_chain.turn_b(0)
    dense_of(2)
    d_chain.turn_b(1)
    dense_of(3)
    d_chain.turn_b(2)
    d_chain.turn_b(3)
    for n in range(4):
        w.wait(tg[n], pair.at[span((x + 2 + n) % 4, DENSE)], partner)

    def g_load(a, b, k):
        px, py = gxy(a, b)
        at = span((px * 4 + py) * 4 + k, 16)
        return g_ref[core, at] + pair[at]

    g_chain = Chain(w, g_load, gto, ga, gb, zh, (ga_out, ga_in, g_small, gb_out, gb_in, g_sum))
    for q in range(4):
        g_chain.begin_a(q)

    tdz = [w.number() for _ in range(3)]
    for q in range(4):
        d_chain.end_b(q)
        if FAR[q]:
            to = device(x, y, (zh + FAR[q]) % 4, zl, core)
            w.start(tdz[FAR[q] - 1], d_sum.at[q], d_zin.at[FAR[q] - 1], to)
    g_chain.turn_b(0)
    for k in (1, 3, 2):
        w.wait(tdz[k - 1], d_zin.at[k - 1], partner)

    def r_block(a, b, k):
        px, py = dxy(a, b)
        return r_ref.at[span((px * 4 + py) * 4 + k, 16)]

    r_block(da, db, zh)[...] = (d_sum[3] + ((d_zin[0] + d_zin[2]) + d_zin[1])).astype(r_ref.dtype)
    back = Spread(w, r_block, dto, da, db, zh, [device(x, y, (zh + k) % 4, zl, core) for k in (1, 3, 2)],
                  [(zh + 4 - k) % 4 for k in (1, 3, 2)])
    back.begin()

    tgz = [[w.number() for _ in range(2)] for _ in range(4)]
    here = [(FAR.index(off), off, dl) for off in FAR for dl in range(2)]
    here = [(q, off, dl) for q, off, dl in here if off or dl]

    def end_g(q):
        g_chain.end_b(q)
        for qq, off, dl in here:
            if qq == q:
                ll = (zl + dl) % 2
                w.start(tgz[off][dl], g_sum.at[q, span(ll, 8)], g_zin.at[off, dl], device(x, y, (zh + off) % 4, ll, core))

    g_chain.turn_b(1)
    g_chain.turn_b(2)
    g_chain.turn_b(3)
    back.take_z(0)
    back.take_b(0)
    end_g(0)
    end_g(1)
    back.take_z(1)
    back.take_z(2)
    end_g(2)
    end_g(3)
    back.take_b(1)
    back.take_b(2)
    back.take_b(3)
    total = g_sum[3, span(zl, 8)]
    for q, off, dl in here:
        w.wait(tgz[off][dl], g_zin.at[off, dl], partner)
        total = total + g_zin[off, dl]
    g_last[...] = total
    ts = w.number()
    w.start(ts, g_last, g_swap, partner)
    for q in range(4):
        back.take_a(q, 0)
    w.wait(ts, g_swap, partner)
    first, second = g_last[...], g_swap[...]
    left = jnp.where(core == 0, first, second)
    right = jnp.where(core == 0, second, first)
    e_ref[:, 0:COLS] = jnp.where(core == 0, left[0:4], left[4:8])
    e_ref[:, COLS:2 * COLS] = jnp.where(core == 0, right[0:4], right[4:8])
    for j in (3, 1, 2):
        for q in range(4):
            back.take_a(q, j)
    w.drain()


def local(entity_table, phases, head_owner, head_row, relation, tail_ids, known_tails):
    messages = 16 + 63 + 24 + 4 + 24 + 3 + 63 + 8 + 1
    here = pl.BlockSpec(memory_space=VMEM)
    e, r = pl.pallas_call(
        step_kernel,
        out_shape=(jax.ShapeDtypeStruct((4, 2 * COLS), F32), jax.ShapeDtypeStruct((1024, COLS), WIRE)),
        in_specs=[here] * 5 + [pl.BlockSpec(memory_space=pltpu.HBM), here],
        out_specs=[here, here],
        scratch_shapes=[
            pltpu.SemaphoreType.DMA((messages,)),
            pltpu.SemaphoreType.DMA((messages,)),
            pltpu.SemaphoreType.DMA,
            pltpu.SemaphoreType.DMA,
            VMEM((1024, COLS), F32),
            VMEM((3, 1024, COLS), BF16),
            VMEM((TRIPLES, COLS), F32),
            VMEM((TRIPLES, COLS), F32),
            VMEM((TRIPLES, STEP), jnp.int32),
            VMEM((TRIPLES, STEP), jnp.int32),
            VMEM((2, 1024, COLS), BF16),
            VMEM((8, 8, STEP), F32),
            VMEM((2, TRIPLES, COLS), BF16),
            VMEM((8, TRIPLES, STEP), BF16),
            VMEM((2, TRIPLES, COLS), BF16),
            VMEM((2, TRIPLES, COLS), BF16),
            VMEM((2, 1024, COLS), F32),
            VMEM((1024, COLS), F32),
            VMEM((1024, COLS), F32),
            VMEM((3, 4, 4, 16, COLS), WIRE),
            VMEM((3, 4, 4, 16, COLS), WIRE),
            VMEM((4, 4, 16, COLS), F32),
            VMEM((3, 4, 16, COLS), WIRE),
            VMEM((3, 4, 16, COLS), WIRE),
            VMEM((4, 16, COLS), F32),
            VMEM((4, 2, 8, COLS), F32),
            VMEM((8, COLS), F32),
            VMEM((8, COLS), F32),
            VMEM((3, 4, 4, 16, COLS), WIRE),
            VMEM((3, 4, 4, 16, COLS), WIRE),
            VMEM((4, 4, 16, COLS), F32),
            VMEM((3, 4, 16, COLS), WIRE),
            VMEM((3, 4, 16, COLS), WIRE),
            VMEM((4, 16, COLS), F32),
            VMEM((3, 16, COLS), F32),
        ],
        compiler_params=pltpu.CompilerParams(collective_id=0, has_side_effects=True, vmem_limit_bytes=36 << 20),
        name="step",
    )(known_tails.T, head_owner.reshape(1, TRIPLES), head_row.reshape(1, TRIPLES), relation.reshape(1, TRIPLES),
      tail_ids.reshape(1, TRIPLES), phases, entity_table)
    return e, r.astype(F32)


def solution(mesh):
    in_specs = (
        P("ent", None),
        P("rel", None),
        P(("ent", "rel"), None),
        P(("ent", "rel")),
        P(("ent", "rel")),
        P(("ent", "rel")),
        P(("ent", "rel"), None),
    )
    out_specs = (P(("ent", "rel"), None), P("rel", None))
    return jax.shard_map(local, mesh=mesh, in_specs=in_specs, out_specs=out_specs, check_vma=False)
```

```python
import functools

import jax
import jax.numpy as jnp
from jax import lax
from jax.experimental import pallas as pl
from jax.experimental.pallas import tpu as pltpu
from jax.sharding import PartitionSpec as P

MESH = pl.DeviceIdType.MESH
VMEM = pltpu.VMEM
F32 = jnp.float32
BF16 = jnp.bfloat16
WIRE = jnp.bfloat16
COLS = 512

SIN = (0.9999999999932018, -0.16666666657817392, 0.008333333144447052, -0.00019841254471923497,
       2.7556704311932283e-06, -2.5038717712098566e-08, 1.5896746642760318e-10, -6.610935072102146e-13)
COS = (0.9999999999990714, -0.4999999999846839, 0.041666666625163704, -0.0013888888455803566,
       2.480156464708791e-05, -2.755665269895137e-07, 2.0865211281170485e-09, -1.1353643820753535e-11,
       4.131574377242709e-14)


def horner(coefficients, t):
    value = jnp.full_like(t, coefficients[-1])
    for c in coefficients[-2::-1]:
        value = value * t + c
    return value


def place():
    e = lax.axis_index("ent")
    r = lax.axis_index("rel")
    return e // 16, (e // 4) % 4, e % 4, r // 2, r % 2


def device(x, y, zh, zl, core):
    return {"ent": x * 16 + y * 4 + zh, "rel": zl * 2 + core}


class Wire:
    def __init__(self, send, recv):
        self.send, self.recv = send, recv
        self.count = 0
        self.open = []

    def number(self):
        self.count += 1
        return self.count - 1

    def start(self, t, src, dst, to):
        copy = pltpu.make_async_remote_copy(
            src_ref=src, dst_ref=dst, send_sem=self.send.at[t], recv_sem=self.recv.at[t],
            device_id=to, device_id_type=MESH)
        copy.start()
        self.open.append(copy)

    def wait(self, t, dst, to):
        pltpu.make_async_remote_copy(
            src_ref=dst, dst_ref=dst, send_sem=self.send.at[t], recv_sem=self.recv.at[t],
            device_id=to, device_id_type=MESH).wait_recv()

    def drain(self):
        for copy in self.open:
            copy.wait_send()
        self.open = []


def greet(x, y, zh, zl, core):
    barrier = pltpu.get_barrier_semaphore()
    z = zh * 2 + zl
    peers = [device(x, y, zh, zl, 1 - core)]
    for d in (1, 2, 3):
        peers.append(device((x + d) % 4, y, zh, zl, core))
        peers.append(device(x, (y + d) % 4, zh, zl, core))
    for d in range(1, 8):
        zz = (z + d) % 8
        peers.append(device(x, y, zz // 2, zz % 2, core))
    for peer in peers:
        pl.semaphore_signal(barrier, inc=1, device_id=peer, device_id_type=MESH)
    return lambda: pl.semaphore_wait(barrier, len(peers))


class Spread:
    def __init__(self, wire, block, to, a0, b0, ks, z_to):
        self.w, self.block, self.to, self.a0, self.b0 = wire, block, to, a0, b0
        self.z_to, self.ks = z_to, ks
        self.tz = [wire.number() for _ in z_to]
        self.tb = [[wire.number() for _ in range(3)] for _ in range(4)]
        self.ta = [[[wire.number() for _ in range(3)] for _ in range(4)] for _ in range(4)]

    def along(self, q, j):
        blk = self.block(self.a0, (self.b0 + j) % 4, self.ks[q])
        for k in (2, 1, 3):
            self.w.start(self.ta[q][j][k - 1], blk, blk, self.to((self.a0 + k) % 4, self.b0))

    def on(self, q):
        blk = self.block(self.a0, self.b0, self.ks[q])
        for k in (2, 1, 3):
            self.w.start(self.tb[q][k - 1], blk, blk, self.to(self.a0, (self.b0 + k) % 4))
        self.along(q, 0)

    def begin(self):
        blk = self.block(self.a0, self.b0, self.ks[0])
        for i in range(3):
            self.w.start(self.tz[i], blk, blk, self.z_to[i])
        self.on(0)

    def take_z(self, i):
        self.w.wait(self.tz[i], self.block(self.a0, self.b0, self.ks[1 + i]), self.z_to[i])
        self.on(1 + i)

    def take_b(self, q):
        for k in (1, 3, 2):
            j = 4 - k
            b = (self.b0 + j) % 4
            self.w.wait(self.tb[q][k - 1], self.block(self.a0, b, self.ks[q]), self.to(self.a0, b))
            self.along(q, j)

    def take_a(self, q, j):
        for k in (1, 3, 2):
            a = (self.a0 + 4 - k) % 4
            self.w.wait(self.ta[q][j][k - 1], self.block(a, (self.b0 + j) % 4, self.ks[q]), self.to(a, self.b0))


FAR = (2, 1, 3, 0)


class Chain:
    def __init__(self, wire, load, to, a0, b0, ks, bufs):
        self.w, self.load, self.to, self.a0, self.b0 = wire, load, to, a0, b0
        self.ks = ks
        self.out_a, self.in_a, self.small, self.out_b, self.in_b, self.last = bufs
        self.ta = [[wire.number() for _ in range(3)] for _ in range(4)]
        self.tb = [[wire.number() for _ in range(3)] for _ in range(4)]

    def piece(self, c, q):
        return jnp.concatenate([self.load(c, b, self.ks[q])[None] for b in range(4)], axis=0)

    def begin_a(self, q):
        for k in (2, 1, 3):
            c = (self.a0 + k) % 4
            self.out_a[k - 1, q] = self.piece(c, q).astype(self.out_a.dtype)
            self.w.start(self.ta[q][k - 1], self.out_a.at[k - 1, q], self.in_a.at[k - 1, q], self.to(c, self.b0))

    def turn_b(self, q):
        for k in (1, 3, 2):
            self.w.wait(self.ta[q][k - 1], self.in_a.at[k - 1, q], self.to((self.a0 + 4 - k) % 4, self.b0))
        near = self.in_a[0, q].astype(F32) + self.in_a[2, q].astype(F32)
        self.small[q] = self.piece(self.a0, q) + (near + self.in_a[1, q].astype(F32))
        for k in (2, 1, 3):
            c = (self.b0 + k) % 4
            self.out_b[k - 1, q] = self.small[q, c].astype(self.out_b.dtype)
            self.w.start(self.tb[q][k - 1], self.out_b.at[k - 1, q], self.in_b.at[k - 1, q], self.to(self.a0, c))

    def end_b(self, q):
        for k in (1, 3, 2):
            self.w.wait(self.tb[q][k - 1], self.in_b.at[k - 1, q], self.to(self.a0, (self.b0 + 4 - k) % 4))
        near = self.in_b[0, q].astype(F32) + self.in_b[2, q].astype(F32)
        self.last[q] = self.small[q, self.b0] + (near + self.in_b[1, q].astype(F32))


def dot(a, b):
    return jnp.dot(a, b, preferred_element_type=F32)


def dot_nt(a, b):
    return lax.dot_general(a, b, (((1,), (1,)), ((), ())), preferred_element_type=F32)


def dot_tn(a, b):
    return lax.dot_general(a, b, (((0,), (0,)), ((), ())), preferred_element_type=F32)


def span(i, n):
    return pl.ds(pl.multiple_of(i * n, n), n)


STEP = 128
MAIN = 512
DENSE = 256
TRIPLES = 512
LISTED = 32


def step_kernel(known_hbm, owner_hbm, place_hbm, relation_hbm, tail_hbm, phases_hbm, entity_hbm, e_ref, r_ref,
                send, recv, local_sem,
                known_ref, owner_ref, place_ref, relation_ref, tail_ref, phases_ref, parts, cos_ref, sin_ref, word_ref, head_ref, table_ref, square_ref,
                query_ref, weight_ref, back_ref, turn_ref, g_ref, pair, d_ref,
                ga_out, ga_in, g_small, gb_out, gb_in, g_sum, g_zin, g_last, g_swap,
                da_out, da_in, d_small, db_out, db_in, d_sum, d_zin):
    x, y, zh, zl, core = place()
    other = 1 - core
    z_sign = 2 * zl - 1
    mine = span(core, COLS)
    theirs = span(other, COLS)
    partner = device(x, y, zh, zl, other)
    w = Wire(send, recv)

    ga, gb = x * other + y * core, y * other + x * core
    da, db = gb, ga

    def gxy(a, b):
        return a * other + b * core, b * other + a * core

    def dxy(a, b):
        return b * other + a * core, a * other + b * core

    def gspan(a, b):
        px, py = gxy(a, b)
        return span(px * 4 + py, 64)

    def dspan(a, b):
        px, py = dxy(a, b)
        return span(px * 4 + py, 64)

    def gto(a, b):
        px, py = gxy(a, b)
        return device(px, py, zh, zl, core)

    def dto(a, b):
        px, py = dxy(a, b)
        return device(px, py, zh, zl, core)

    everyone = greet(x, y, zh, zl, core)

    tp = [w.number() for _ in range(16)]

    def block(a, b, k):
        px, py = gxy(a, b)
        return table_ref.at[core, span((px * 4 + py) * 4 + k, 16)]

    z_to = [device(x, y, (zh + z_sign + 4) % 4, 1 - zl, core), device(x, y, (zh + z_sign + 4) % 4, zl, core),
            device(x, y, (zh + 2) % 4, 1 - zl, core)]
    z_from = [(zh + z_sign + 4) % 4, (zh - z_sign + 4) % 4, (zh + 2) % 4]
    own = pltpu.make_async_copy(entity_hbm.at[:, mine], block(ga, gb, zh), local_sem.at[0])
    own.start()
    pairs = ((phases_hbm, phases_ref), (known_hbm, known_ref), (owner_hbm, owner_ref), (place_hbm, place_ref),
             (relation_hbm, relation_ref), (tail_hbm, tail_ref))
    fetches = [pltpu.make_async_copy(a, b, local_sem.at[1 + i]) for i, (a, b) in enumerate(pairs)]
    for f in fetches:
        f.start()
    own.wait()
    everyone()
    spread = Spread(w, block, gto, ga, gb, [zh] + z_from, z_to)
    spread.begin()

    def push(i, a, b):
        part = table_ref.at[core, gspan(a, b)]
        w.start(tp[i], part, part, partner)

    for f in fetches:
        f.wait()

    def split(i, _):
        at = span(i, STEP)
        p = phases_ref[at]
        for k in range(3):
            q = p.astype(BF16)
            parts[k, at] = q
            p = p - q.astype(F32)
        return 0

    lax.fori_loop(0, 8, split, 0)

    lane = lax.broadcasted_iota(jnp.int32, (1, STEP), 1)

    def down(row):
        return jnp.transpose(jnp.broadcast_to(row, (STEP, STEP)))

    def hot_rows(col):
        return jnp.concatenate([(col == lane + 128 * k).astype(F32).astype(BF16) for k in range(8)], axis=1)

    def prepare(i, _):
        at = span(i, STEP)
        head_ref[at] = down(owner_ref[:, at] * 4 + place_ref[:, at])
        hot = hot_rows(down(relation_ref[:, at]))
        angle = dot(hot, parts[0]) + dot(hot, parts[1]) + dot(hot, parts[2])
        t = angle * angle
        cos_ref[at] = horner(COS, t)
        sin_ref[at] = angle * horner(SIN, t)
        ids = jnp.transpose(known_ref[:, at])
        low = ids & 127
        bit = jnp.left_shift(jnp.int32(1), jnp.right_shift(ids, 7))
        word = jnp.zeros((STEP, STEP), jnp.int32)
        for j in range(LISTED):
            word = word | jnp.where(low[:, j:j + 1] == lane, bit[:, j:j + 1], 0)
        tail = down(tail_ref[:, at])
        keep = jnp.where((tail & 127) == lane, jnp.left_shift(jnp.int32(1), jnp.right_shift(tail, 7)), 0)
        word_ref[at] = (word & ~keep) | jnp.left_shift(keep, 8)
        return 0

    spread.take_z(0)
    spread.take_b(0)
    lax.fori_loop(0, 1, prepare, 0)
    spread.take_z(1)
    spread.take_z(2)
    lax.fori_loop(1, 2, prepare, 0)
    for q in (1, 2, 3):
        spread.take_b(q)
    for j in range(4):
        push(j, ga, (gb + j) % 4)
    lax.fori_loop(2, 4, prepare, 0)
    for j in (0, 3, 1, 2):
        for q in range(4):
            spread.take_a(q, j)
        for k in (1, 3, 2):
            push(4 * k + j, (ga + 4 - k) % 4, (gb + j) % 4)
    for i in range(16):
        w.wait(tp[i], table_ref.at[other, pl.ds(0, 64)], partner)

    def squares(i, _):
        re, im = table_ref[0, span(i, STEP)].astype(F32), table_ref[1, span(i, STEP)].astype(F32)
        s = jnp.sum(re * re + im * im, axis=1, keepdims=True)
        square_ref[i] = jnp.transpose(jnp.broadcast_to(s, (STEP, STEP)))[0:8]
        return 0

    lax.fori_loop(0, 8, squares, 0)

    def main(i, _):
        at = span(i, MAIN)
        hot = hot_rows(head_ref[at])
        c, s = cos_ref[at], sin_ref[at]
        hr, hm = dot(hot, table_ref[0]), dot(hot, table_ref[1])
        qr = hr * c - hm * s
        qm = hr * s + hm * c
        query_r, query_m = qr.astype(BF16), qm.astype(BF16)
        query_ref[0, at] = query_r
        query_ref[1, at] = query_m
        near_r, near_m = query_r.astype(F32), query_m.astype(F32)
        query_sq = jnp.sum(near_r * near_r + near_m * near_m, axis=1, keepdims=True)
        cross = dot_nt(query_r, table_ref[0]) + dot_nt(query_m, table_ref[1])
        word = word_ref[at]
        scores, hidden = [], []
        top = None
        for k in range(8):
            sc = 2.0 * cross[:, k * 128:(k + 1) * 128] - query_sq - square_ref[k, 0:1]
            hide = (word & (1 << k)) != 0
            scores.append(sc)
            hidden.append(hide)
            seen = jnp.where(hide, -jnp.inf, sc)
            top = seen if top is None else jnp.maximum(top, seen)
        top = jnp.max(top, axis=1, keepdims=True)
        raws = []
        for k in range(8):
            raws.append(jnp.where(hidden[k], 0.0, jnp.exp(scores[k] - top)))
        total = raws[0]
        for k in range(1, 8):
            total = total + raws[k]
        scale = 2.0 / jnp.sum(total, axis=1, keepdims=True)
        weights = []
        for k in range(8):
            hit = (word & (256 << k)) != 0
            wk = (raws[k] * scale - jnp.where(hit, 2.0, 0.0)).astype(BF16)
            weights.append(wk)
            weight_ref[k, at] = wk
        both = jnp.concatenate(weights, axis=1)
        gr, gm = dot(both, table_ref[0]), dot(both, table_ref[1])
        back_ref[0, at] = (gr * c + gm * s).astype(BF16)
        back_ref[1, at] = (gm * c - gr * s).astype(BF16)
        turn = qr * gm - qm * gr
        high = turn.astype(BF16)
        turn_ref[0, at] = high
        turn_ref[1, at] = (turn - high.astype(F32)).astype(BF16)
        return 0

    lax.fori_loop(0, TRIPLES // MAIN, main, 0)

    def key(i):
        return lax.broadcasted_iota(jnp.int32, (DENSE, 1), 0) + i * DENSE

    def relations(i, _):
        hot = (relation_ref[...] == key(i)).astype(F32).astype(BF16)
        d_ref[span(i, DENSE)] = dot(hot, turn_ref[0]) + dot(hot, turn_ref[1])
        return 0

    lax.fori_loop(0, 1024 // DENSE, relations, 0)

    def d_load(a, b, k):
        px, py = dxy(a, b)
        return d_ref[span((px * 4 + py) * 4 + k, 16)]

    d_chain = Chain(w, d_load, dto, da, db, list(range(4)), (da_out, da_in, d_small, db_out, db_in, d_sum))
    for q in range(4):
        d_chain.begin_a(q)

    ones = jnp.ones((TRIPLES, 128), BF16)
    heads = owner_ref[...] * 4 + place_ref[...]

    def dense(i):
        at = span(i, DENSE)
        wk = jnp.concatenate([weight_ref[i * (DENSE // 128) + k] for k in range(DENSE // 128)], axis=1)
        counts = dot_tn(wk, ones)
        hot = (heads == key(i)).astype(F32).astype(BF16)
        many = jnp.concatenate([counts] * 4, axis=1)
        for c in range(2):
            sums = dot_tn(wk, query_ref[c]) + dot(hot, back_ref[c])
            g_ref[c, at] = sums - many * table_ref[c, at].astype(F32)

    tg = [w.number() for _ in range(4)]

    def dense_of(n):
        i = (x + 2 + n) % 4
        dense(i)
        w.start(tg[n], g_ref.at[other, span(i, DENSE)], pair.at[span(i, DENSE)], partner)

    tdz = [[w.number() for _ in range(3)] for _ in range(4)]

    def share(q):
        d_chain.end_b(q)
        d_zin[zh, q] = d_sum[q].astype(d_zin.dtype)
        for k in (2, 1, 3):
            to = device(x, y, (zh + k) % 4, zl, core)
            w.start(tdz[q][k - 1], d_zin.at[zh, q], d_zin.at[zh, q], to)

    def r_block(a, b, k):
        px, py = dxy(a, b)
        return r_ref.at[span((px * 4 + py) * 4 + k, 16)]

    back = Spread(w, r_block, dto, da, db, list(range(4)), [])

    def settle(q):
        for k in (1, 3, 2):
            w.wait(tdz[q][k - 1], d_zin.at[(zh + 4 - k) % 4, q], partner)
        z = [d_zin[k, q].astype(F32) for k in range(4)]
        r_block(da, db, q)[...] = ((z[0] + z[1]) + (z[2] + z[3])).astype(r_ref.dtype)
        back.on(q)

    dense_of(0)
    dense_of(1)
    d_chain.turn_b(0)
    dense_of(2)
    d_chain.turn_b(1)
    share(0)
    dense_of(3)
    d_chain.turn_b(2)
    share(1)
    d_chain.turn_b(3)
    share(2)

    def g_load(a, b, k):
        px, py = gxy(a, b)
        at = span((px * 4 + py) * 4 + k, 16)
        return g_ref[core, at] + pair[at]

    g_chain = Chain(w, g_load, gto, ga, gb, [(zh + off) % 4 for off in FAR],
                    (ga_out, ga_in, g_small, gb_out, gb_in, g_sum))
    for n in range(4):
        w.wait(tg[n], pair.at[span((x + 2 + n) % 4, DENSE)], partner)
    g_chain.begin_a(0)
    g_chain.begin_a(1)
    share(3)
    settle(0)
    g_chain.begin_a(2)
    g_chain.begin_a(3)

    tgz = [[w.number() for _ in range(2)] for _ in range(4)]
    here = [(FAR.index(off), off, dl) for off in FAR for dl in range(2)]
    here = [(q, off, dl) for q, off, dl in here if off or dl]

    def end_g(q):
        g_chain.end_b(q)
        for qq, off, dl in here:
            if qq == q:
                ll = (zl + dl) % 2
                w.start(tgz[off][dl], g_sum.at[q, span(ll, 8)], g_zin.at[off, dl], device(x, y, (zh + off) % 4, ll, core))

    settle(1)
    settle(2)
    g_chain.turn_b(0)
    settle(3)
    back.take_b(0)
    g_chain.turn_b(1)
    back.take_b(1)
    g_chain.turn_b(2)
    back.take_b(2)
    g_chain.turn_b(3)
    end_g(0)
    back.take_b(3)
    end_g(1)
    end_g(2)
    end_g(3)
    total = g_sum[3, span(zl, 8)]
    for q, off, dl in here:
        w.wait(tgz[off][dl], g_zin.at[off, dl], partner)
        total = total + g_zin[off, dl]
    g_last[...] = total
    ts = w.number()
    w.start(ts, g_last, g_swap, partner)
    for q in range(4):
        back.take_a(q, 0)
    w.wait(ts, g_swap, partner)
    first, second = g_last[...], g_swap[...]
    left = jnp.where(core == 0, first, second)
    right = jnp.where(core == 0, second, first)
    e_ref[:, 0:COLS] = jnp.where(core == 0, left[0:4], left[4:8])
    e_ref[:, COLS:2 * COLS] = jnp.where(core == 0, right[0:4], right[4:8])
    for j in (3, 1, 2):
        for q in range(4):
            back.take_a(q, j)
    w.drain()


def local(entity_table, phases, head_owner, head_row, relation, tail_ids, known_tails):
    messages = 16 + 63 + 24 + 4 + 24 + 12 + 60 + 8 + 1
    here = pl.BlockSpec(memory_space=VMEM)
    e, r = pl.pallas_call(
        step_kernel,
        out_shape=(jax.ShapeDtypeStruct((4, 2 * COLS), F32), jax.ShapeDtypeStruct((1024, COLS), WIRE)),
        in_specs=[pl.BlockSpec(memory_space=pltpu.HBM)] * 7,
        out_specs=[here, here],
        scratch_shapes=[
            pltpu.SemaphoreType.DMA((messages,)),
            pltpu.SemaphoreType.DMA((messages,)),
            pltpu.SemaphoreType.DMA((7,)),
            VMEM((LISTED, TRIPLES), jnp.int32),
            VMEM((1, TRIPLES), jnp.int32),
            VMEM((1, TRIPLES), jnp.int32),
            VMEM((1, TRIPLES), jnp.int32),
            VMEM((1, TRIPLES), jnp.int32),
            VMEM((1024, COLS), F32),
            VMEM((3, 1024, COLS), BF16),
            VMEM((TRIPLES, COLS), F32),
            VMEM((TRIPLES, COLS), F32),
            VMEM((TRIPLES, STEP), jnp.int32),
            VMEM((TRIPLES, STEP), jnp.int32),
            VMEM((2, 1024, COLS), BF16),
            VMEM((8, 8, STEP), F32),
            VMEM((2, TRIPLES, COLS), BF16),
            VMEM((8, TRIPLES, STEP), BF16),
            VMEM((2, TRIPLES, COLS), BF16),
            VMEM((2, TRIPLES, COLS), BF16),
            VMEM((2, 1024, COLS), F32),
            VMEM((1024, COLS), F32),
            VMEM((1024, COLS), F32),
            VMEM((3, 4, 4, 16, COLS), WIRE),
            VMEM((3, 4, 4, 16, COLS), WIRE),
            VMEM((4, 4, 16, COLS), F32),
            VMEM((3, 4, 16, COLS), WIRE),
            VMEM((3, 4, 16, COLS), WIRE),
            VMEM((4, 16, COLS), F32),
            VMEM((4, 2, 8, COLS), F32),
            VMEM((8, COLS), F32),
            VMEM((8, COLS), F32),
            VMEM((3, 4, 4, 16, COLS), WIRE),
            VMEM((3, 4, 4, 16, COLS), WIRE),
            VMEM((4, 4, 16, COLS), F32),
            VMEM((3, 4, 16, COLS), WIRE),
            VMEM((3, 4, 16, COLS), WIRE),
            VMEM((4, 16, COLS), F32),
            VMEM((4, 4, 16, COLS), WIRE),
        ],
        compiler_params=pltpu.CompilerParams(collective_id=0, has_side_effects=True, vmem_limit_bytes=36 << 20),
        name="step",
    )(*(pltpu.with_memory_space_constraint(v, pltpu.HBM) for v in (
        known_tails.T, head_owner.reshape(1, TRIPLES), head_row.reshape(1, TRIPLES), relation.reshape(1, TRIPLES),
        tail_ids.reshape(1, TRIPLES), phases, entity_table)))
    return e, r.astype(F32)


def solution(mesh):
    in_specs = (
        P("ent", None),
        P("rel", None),
        P(("ent", "rel"), None),
        P(("ent", "rel")),
        P(("ent", "rel")),
        P(("ent", "rel")),
        P(("ent", "rel"), None),
    )
    out_specs = (P(("ent", "rel"), None), P("rel", None))
    return jax.shard_map(local, mesh=mesh, in_specs=in_specs, out_specs=out_specs, check_vma=False)
```

```python
import functools

import jax
import jax.numpy as jnp
from jax import lax
from jax.experimental import pallas as pl
from jax.experimental.pallas import tpu as pltpu
from jax.sharding import PartitionSpec as P

MESH = pl.DeviceIdType.MESH
VMEM = pltpu.VMEM
F32 = jnp.float32
BF16 = jnp.bfloat16
WIRE = jnp.bfloat16
COLS = 512

SIN = (0.9999999999932018, -0.16666666657817392, 0.008333333144447052, -0.00019841254471923497,
       2.7556704311932283e-06, -2.5038717712098566e-08, 1.5896746642760318e-10, -6.610935072102146e-13)
COS = (0.9999999999990714, -0.4999999999846839, 0.041666666625163704, -0.0013888888455803566,
       2.480156464708791e-05, -2.755665269895137e-07, 2.0865211281170485e-09, -1.1353643820753535e-11,
       4.131574377242709e-14)


def horner(coefficients, t):
    value = jnp.full_like(t, coefficients[-1])
    for c in coefficients[-2::-1]:
        value = value * t + c
    return value


def place():
    e = lax.axis_index("ent")
    r = lax.axis_index("rel")
    return e // 16, (e // 4) % 4, e % 4, r // 2, r % 2


def device(x, y, zh, zl, core):
    return {"ent": x * 16 + y * 4 + zh, "rel": zl * 2 + core}


class Wire:
    def __init__(self, send, recv):
        self.send, self.recv = send, recv
        self.count = 0
        self.open = []

    def number(self):
        self.count += 1
        return self.count - 1

    def start(self, t, src, dst, to):
        copy = pltpu.make_async_remote_copy(
            src_ref=src, dst_ref=dst, send_sem=self.send.at[t], recv_sem=self.recv.at[t],
            device_id=to, device_id_type=MESH)
        copy.start()
        self.open.append(copy)

    def wait(self, t, dst, to):
        pltpu.make_async_remote_copy(
            src_ref=dst, dst_ref=dst, send_sem=self.send.at[t], recv_sem=self.recv.at[t],
            device_id=to, device_id_type=MESH).wait_recv()

    def drain(self):
        for copy in self.open:
            copy.wait_send()
        self.open = []


def greet(x, y, zh, zl, core):
    barrier = pltpu.get_barrier_semaphore()
    z = zh * 2 + zl
    peers = [device(x, y, zh, zl, 1 - core)]
    for d in (1, 2, 3):
        peers.append(device((x + d) % 4, y, zh, zl, core))
        peers.append(device(x, (y + d) % 4, zh, zl, core))
    for d in range(1, 8):
        zz = (z + d) % 8
        peers.append(device(x, y, zz // 2, zz % 2, core))
    for peer in peers:
        pl.semaphore_signal(barrier, inc=1, device_id=peer, device_id_type=MESH)
    return lambda: pl.semaphore_wait(barrier, len(peers))


class Spread:
    def __init__(self, wire, block, to, a0, b0, ks, z_to):
        self.w, self.block, self.to, self.a0, self.b0 = wire, block, to, a0, b0
        self.z_to, self.ks = z_to, ks
        self.tz = [wire.number() for _ in z_to]
        self.tb = [[wire.number() for _ in range(3)] for _ in range(4)]
        self.ta = [[[wire.number() for _ in range(3)] for _ in range(4)] for _ in range(4)]

    def along(self, q, j):
        blk = self.block(self.a0, (self.b0 + j) % 4, self.ks[q])
        for k in (2, 1, 3):
            self.w.start(self.ta[q][j][k - 1], blk, blk, self.to((self.a0 + k) % 4, self.b0))

    def on(self, q):
        blk = self.block(self.a0, self.b0, self.ks[q])
        for k in (2, 1, 3):
            self.w.start(self.tb[q][k - 1], blk, blk, self.to(self.a0, (self.b0 + k) % 4))
        self.along(q, 0)

    def begin(self):
        blk = self.block(self.a0, self.b0, self.ks[0])
        for i in range(3):
            self.w.start(self.tz[i], blk, blk, self.z_to[i])
        self.on(0)

    def take_z(self, i):
        self.w.wait(self.tz[i], self.block(self.a0, self.b0, self.ks[1 + i]), self.z_to[i])
        self.on(1 + i)

    def take_b(self, q):
        for k in (1, 3, 2):
            j = 4 - k
            b = (self.b0 + j) % 4
            self.w.wait(self.tb[q][k - 1], self.block(self.a0, b, self.ks[q]), self.to(self.a0, b))
            self.along(q, j)

    def take_a(self, q, j):
        for k in (1, 3, 2):
            a = (self.a0 + 4 - k) % 4
            self.w.wait(self.ta[q][j][k - 1], self.block(a, (self.b0 + j) % 4, self.ks[q]), self.to(a, self.b0))


FAR = (2, 1, 3, 0)


class Chain:
    def __init__(self, wire, load, to, a0, b0, ks, bufs):
        self.w, self.load, self.to, self.a0, self.b0 = wire, load, to, a0, b0
        self.ks = ks
        self.out_a, self.in_a, self.small, self.out_b, self.in_b, self.last = bufs
        self.ta = [[wire.number() for _ in range(3)] for _ in range(4)]
        self.tb = [[wire.number() for _ in range(3)] for _ in range(4)]

    def piece(self, c, q):
        return jnp.concatenate([self.load(c, b, self.ks[q])[None] for b in range(4)], axis=0)

    def begin_a(self, q):
        for k in (2, 1, 3):
            c = (self.a0 + k) % 4
            self.out_a[k - 1, q] = self.piece(c, q).astype(self.out_a.dtype)
            self.w.start(self.ta[q][k - 1], self.out_a.at[k - 1, q], self.in_a.at[k - 1, q], self.to(c, self.b0))

    def turn_b(self, q):
        for k in (1, 3, 2):
            self.w.wait(self.ta[q][k - 1], self.in_a.at[k - 1, q], self.to((self.a0 + 4 - k) % 4, self.b0))
        near = self.in_a[0, q].astype(F32) + self.in_a[2, q].astype(F32)
        self.small[q] = self.piece(self.a0, q) + (near + self.in_a[1, q].astype(F32))
        for k in (2, 1, 3):
            c = (self.b0 + k) % 4
            self.out_b[k - 1, q] = self.small[q, c].astype(self.out_b.dtype)
            self.w.start(self.tb[q][k - 1], self.out_b.at[k - 1, q], self.in_b.at[k - 1, q], self.to(self.a0, c))

    def end_b(self, q):
        for k in (1, 3, 2):
            self.w.wait(self.tb[q][k - 1], self.in_b.at[k - 1, q], self.to(self.a0, (self.b0 + 4 - k) % 4))
        near = self.in_b[0, q].astype(F32) + self.in_b[2, q].astype(F32)
        self.last[q] = self.small[q, self.b0] + (near + self.in_b[1, q].astype(F32))


def dot(a, b):
    return jnp.dot(a, b, preferred_element_type=F32)


def dot_nt(a, b):
    return lax.dot_general(a, b, (((1,), (1,)), ((), ())), preferred_element_type=F32)


def dot_tn(a, b):
    return lax.dot_general(a, b, (((0,), (0,)), ((), ())), preferred_element_type=F32)


def span(i, n):
    return pl.ds(pl.multiple_of(i * n, n), n)


STEP = 128
MAIN = 512
DENSE = 256
TRIPLES = 512
LISTED = 32


def step_kernel(known_hbm, owner_hbm, place_hbm, relation_hbm, tail_hbm, phases_hbm, entity_hbm, e_ref, r_ref,
                send, recv, local_sem,
                known_ref, owner_ref, place_ref, relation_ref, tail_ref, phases_ref, parts, cos_ref, sin_ref, word_ref, head_ref, table_ref, square_ref,
                query_ref, weight_ref, back_ref, turn_ref, g_ref, pair, d_ref,
                ga_out, ga_in, g_small, gb_out, gb_in, g_sum, g_zin, g_last, g_swap,
                da_out, da_in, d_small, db_out, db_in, d_sum, d_zin):
    x, y, zh, zl, core = place()
    other = 1 - core
    z_sign = 2 * zl - 1
    mine = span(core, COLS)
    theirs = span(other, COLS)
    partner = device(x, y, zh, zl, other)
    w = Wire(send, recv)

    ga, gb = x * other + y * core, y * other + x * core
    da, db = gb, ga

    def gxy(a, b):
        return a * other + b * core, b * other + a * core

    def dxy(a, b):
        return b * other + a * core, a * other + b * core

    def gspan(a, b):
        px, py = gxy(a, b)
        return span(px * 4 + py, 64)

    def dspan(a, b):
        px, py = dxy(a, b)
        return span(px * 4 + py, 64)

    def gto(a, b):
        px, py = gxy(a, b)
        return device(px, py, zh, zl, core)

    def dto(a, b):
        px, py = dxy(a, b)
        return device(px, py, zh, zl, core)

    everyone = greet(x, y, zh, zl, core)

    tp = [w.number() for _ in range(16)]

    def block(a, b, k):
        px, py = gxy(a, b)
        return table_ref.at[core, span((px * 4 + py) * 4 + k, 16)]

    z_to = [device(x, y, (zh + z_sign + 4) % 4, 1 - zl, core), device(x, y, (zh + z_sign + 4) % 4, zl, core),
            device(x, y, (zh + 2) % 4, 1 - zl, core)]
    z_from = [(zh + z_sign + 4) % 4, (zh - z_sign + 4) % 4, (zh + 2) % 4]
    own = pltpu.make_async_copy(entity_hbm.at[:, mine], block(ga, gb, zh), local_sem.at[0])
    own.start()
    pairs = ((phases_hbm, phases_ref), (known_hbm, known_ref), (owner_hbm, owner_ref), (place_hbm, place_ref),
             (relation_hbm, relation_ref), (tail_hbm, tail_ref))
    fetches = [pltpu.make_async_copy(a, b, local_sem.at[1 + i]) for i, (a, b) in enumerate(pairs)]
    for f in fetches:
        f.start()
    own.wait()
    everyone()
    spread = Spread(w, block, gto, ga, gb, [zh] + z_from, z_to)
    spread.begin()

    def push(i, a, b):
        part = table_ref.at[core, gspan(a, b)]
        w.start(tp[i], part, part, partner)

    for f in fetches:
        f.wait()

    def split(i, _):
        at = span(i, STEP)
        p = phases_ref[at]
        for k in range(3):
            q = p.astype(BF16)
            parts[k, at] = q
            p = p - q.astype(F32)
        return 0

    lax.fori_loop(0, 8, split, 0)

    lane = lax.broadcasted_iota(jnp.int32, (1, STEP), 1)

    def down(row):
        return jnp.transpose(jnp.broadcast_to(row, (STEP, STEP)))

    def hot_rows(col):
        return jnp.concatenate([(col == lane + 128 * k).astype(F32).astype(BF16) for k in range(8)], axis=1)

    def prepare(i, _):
        at = span(i, STEP)
        head_ref[at] = down(owner_ref[:, at] * 4 + place_ref[:, at])
        hot = hot_rows(down(relation_ref[:, at]))
        angle = dot(hot, parts[0]) + dot(hot, parts[1]) + dot(hot, parts[2])
        t = angle * angle
        cos_ref[at] = horner(COS, t)
        sin_ref[at] = angle * horner(SIN, t)
        ids = jnp.transpose(known_ref[:, at])
        low = ids & 127
        bit = jnp.left_shift(jnp.int32(1), jnp.right_shift(ids, 7))
        word = jnp.zeros((STEP, STEP), jnp.int32)
        for j in range(LISTED):
            word = word | jnp.where(low[:, j:j + 1] == lane, bit[:, j:j + 1], 0)
        tail = down(tail_ref[:, at])
        keep = jnp.where((tail & 127) == lane, jnp.left_shift(jnp.int32(1), jnp.right_shift(tail, 7)), 0)
        word_ref[at] = (word & ~keep) | jnp.left_shift(keep, 8)
        return 0

    spread.take_z(0)
    spread.take_b(0)
    lax.fori_loop(0, 1, prepare, 0)
    spread.take_z(1)
    spread.take_z(2)
    lax.fori_loop(1, 2, prepare, 0)
    for q in (1, 2, 3):
        spread.take_b(q)
    for j in range(4):
        push(j, ga, (gb + j) % 4)
    lax.fori_loop(2, 4, prepare, 0)
    for j in (0, 3, 1, 2):
        for q in range(4):
            spread.take_a(q, j)
        for k in (1, 3, 2):
            push(4 * k + j, (ga + 4 - k) % 4, (gb + j) % 4)
    for i in range(16):
        w.wait(tp[i], table_ref.at[other, pl.ds(0, 64)], partner)

    def squares(i, _):
        re, im = table_ref[0, span(i, STEP)].astype(F32), table_ref[1, span(i, STEP)].astype(F32)
        s = jnp.sum(re * re + im * im, axis=1, keepdims=True)
        square_ref[i] = jnp.transpose(jnp.broadcast_to(s, (STEP, STEP)))[0:8]
        return 0

    lax.fori_loop(0, 8, squares, 0)

    def main(i, _):
        at = span(i, MAIN)
        hot = hot_rows(head_ref[at])
        c, s = cos_ref[at], sin_ref[at]
        hr, hm = dot(hot, table_ref[0]), dot(hot, table_ref[1])
        qr = hr * c - hm * s
        qm = hr * s + hm * c
        query_r, query_m = qr.astype(BF16), qm.astype(BF16)
        query_ref[0, at] = query_r
        query_ref[1, at] = query_m
        near_r, near_m = query_r.astype(F32), query_m.astype(F32)
        query_sq = jnp.sum(near_r * near_r + near_m * near_m, axis=1, keepdims=True)
        cross = dot_nt(query_r, table_ref[0]) + dot_nt(query_m, table_ref[1])
        word = word_ref[at]
        scores, hidden = [], []
        top = None
        for k in range(8):
            sc = 2.0 * cross[:, k * 128:(k + 1) * 128] - query_sq - square_ref[k, 0:1]
            hide = (word & (1 << k)) != 0
            scores.append(sc)
            hidden.append(hide)
            seen = jnp.where(hide, -jnp.inf, sc)
            top = seen if top is None else jnp.maximum(top, seen)
        top = jnp.max(top, axis=1, keepdims=True)
        raws = []
        for k in range(8):
            raws.append(jnp.where(hidden[k], 0.0, jnp.exp(scores[k] - top)))
        total = raws[0]
        for k in range(1, 8):
            total = total + raws[k]
        scale = 2.0 / jnp.sum(total, axis=1, keepdims=True)
        weights = []
        for k in range(8):
            hit = (word & (256 << k)) != 0
            wk = (raws[k] * scale - jnp.where(hit, 2.0, 0.0)).astype(BF16)
            weights.append(wk)
            weight_ref[k, at] = wk
        both = jnp.concatenate(weights, axis=1)
        gr, gm = dot(both, table_ref[0]), dot(both, table_ref[1])
        back_ref[0, at] = (gr * c + gm * s).astype(BF16)
        back_ref[1, at] = (gm * c - gr * s).astype(BF16)
        turn = qr * gm - qm * gr
        high = turn.astype(BF16)
        turn_ref[0, at] = high
        turn_ref[1, at] = (turn - high.astype(F32)).astype(BF16)
        return 0

    lax.fori_loop(0, TRIPLES // MAIN, main, 0)

    def key(i):
        return lax.broadcasted_iota(jnp.int32, (DENSE, 1), 0) + i * DENSE

    def relations(i, _):
        hot = (relation_ref[...] == key(i)).astype(F32).astype(BF16)
        d_ref[span(i, DENSE)] = dot(hot, turn_ref[0]) + dot(hot, turn_ref[1])
        return 0

    lax.fori_loop(0, 1024 // DENSE, relations, 0)

    def d_load(a, b, k):
        px, py = dxy(a, b)
        return d_ref[span((px * 4 + py) * 4 + k, 16)]

    d_chain = Chain(w, d_load, dto, da, db, list(range(4)), (da_out, da_in, d_small, db_out, db_in, d_sum))
    for q in range(4):
        d_chain.begin_a(q)

    ones = jnp.ones((TRIPLES, 128), BF16)
    heads = owner_ref[...] * 4 + place_ref[...]

    def dense(i):
        at = span(i, DENSE)
        wk = jnp.concatenate([weight_ref[i * (DENSE // 128) + k] for k in range(DENSE // 128)], axis=1)
        counts = dot_tn(wk, ones)
        hot = (heads == key(i)).astype(F32).astype(BF16)
        many = jnp.concatenate([counts] * 4, axis=1)
        for c in range(2):
            sums = dot_tn(wk, query_ref[c]) + dot(hot, back_ref[c])
            g_ref[c, at] = sums - many * table_ref[c, at].astype(F32)

    tg = [w.number() for _ in range(4)]

    def dense_of(n):
        i = (x + 2 + n) % 4
        dense(i)
        w.start(tg[n], g_ref.at[other, span(i, DENSE)], pair.at[span(i, DENSE)], partner)

    tdz = [[w.number() for _ in range(3)] for _ in range(4)]

    def share(q):
        d_chain.end_b(q)
        d_zin[zh, q] = d_sum[q].astype(d_zin.dtype)
        for k in (2, 1, 3):
            to = device(x, y, (zh + k) % 4, zl, core)
            w.start(tdz[q][k - 1], d_zin.at[zh, q], d_zin.at[zh, q], to)

    def r_block(a, b, k):
        px, py = dxy(a, b)
        return r_ref.at[span((px * 4 + py) * 4 + k, 16)]

    back = Spread(w, r_block, dto, da, db, list(range(4)), [])

    def settle(q):
        for k in (1, 3, 2):
            w.wait(tdz[q][k - 1], d_zin.at[(zh + 4 - k) % 4, q], partner)
        z = [d_zin[k, q].astype(F32) for k in range(4)]
        r_block(da, db, q)[...] = ((z[0] + z[1]) + (z[2] + z[3])).astype(r_ref.dtype)
        back.on(q)

    def g_load(a, b, k):
        px, py = gxy(a, b)
        at = span((px * 4 + py) * 4 + k, 16)
        return g_ref[core, at] + pair[at]

    g_chain = Chain(w, g_load, gto, ga, gb, [(zh + off) % 4 for off in FAR],
                    (ga_out, ga_in, g_small, gb_out, gb_in, g_sum))
    tgz = [[w.number() for _ in range(2)] for _ in range(4)]
    here = [(FAR.index(off), off, dl) for off in FAR for dl in range(2)]
    here = [(q, off, dl) for q, off, dl in here if off or dl]

    def end_g(q):
        g_chain.end_b(q)
        for qq, off, dl in here:
            if qq == q:
                ll = (zl + dl) % 2
                w.start(tgz[off][dl], g_sum.at[q, span(ll, 8)], g_zin.at[off, dl], device(x, y, (zh + off) % 4, ll, core))

    ts = w.number()

    def pairs_in():
        for n in range(4):
            w.wait(tg[n], pair.at[span((x + 2 + n) % 4, DENSE)], partner)

    def send_last():
        total = g_sum[3, span(zl, 8)]
        for q, off, dl in here:
            w.wait(tgz[off][dl], g_zin.at[off, dl], partner)
            total = total + g_zin[off, dl]
        g_last[...] = total
        w.start(ts, g_last, g_swap, partner)

    def finish():
        w.wait(ts, g_swap, partner)
        first, second = g_last[...], g_swap[...]
        left = jnp.where(core == 0, first, second)
        right = jnp.where(core == 0, second, first)
        e_ref[:, 0:COLS] = jnp.where(core == 0, left[0:4], left[4:8])
        e_ref[:, COLS:2 * COLS] = jnp.where(core == 0, right[0:4], right[4:8])

    def ahead(j):
        for q in range(4):
            back.take_a(q, j)

    dense_of(0)
    dense_of(1)
    dense_of(2)
    dense_of(3)
    d_chain.turn_b(0)
    d_chain.turn_b(1)
    pairs_in()
    g_chain.begin_a(0)
    g_chain.begin_a(1)
    d_chain.turn_b(2)
    d_chain.turn_b(3)
    g_chain.begin_a(2)
    g_chain.begin_a(3)
    share(0)
    share(1)
    share(2)
    share(3)
    g_chain.turn_b(0)
    g_chain.turn_b(1)
    g_chain.turn_b(2)
    g_chain.turn_b(3)
    settle(0)
    settle(1)
    settle(2)
    settle(3)
    back.take_b(0)
    end_g(0)
    back.take_b(1)
    end_g(1)
    back.take_b(2)
    end_g(2)
    back.take_b(3)
    end_g(3)
    send_last()
    finish()
    ahead(0)
    ahead(3)
    ahead(1)
    ahead(2)
    w.drain()


def local(entity_table, phases, head_owner, head_row, relation, tail_ids, known_tails):
    messages = 16 + 63 + 24 + 4 + 24 + 12 + 60 + 8 + 1
    here = pl.BlockSpec(memory_space=VMEM)
    e, r = pl.pallas_call(
        step_kernel,
        out_shape=(jax.ShapeDtypeStruct((4, 2 * COLS), F32), jax.ShapeDtypeStruct((1024, COLS), WIRE)),
        in_specs=[pl.BlockSpec(memory_space=pltpu.HBM)] * 7,
        out_specs=[here, here],
        scratch_shapes=[
            pltpu.SemaphoreType.DMA((messages,)),
            pltpu.SemaphoreType.DMA((messages,)),
            pltpu.SemaphoreType.DMA((7,)),
            VMEM((LISTED, TRIPLES), jnp.int32),
            VMEM((1, TRIPLES), jnp.int32),
            VMEM((1, TRIPLES), jnp.int32),
            VMEM((1, TRIPLES), jnp.int32),
            VMEM((1, TRIPLES), jnp.int32),
            VMEM((1024, COLS), F32),
            VMEM((3, 1024, COLS), BF16),
            VMEM((TRIPLES, COLS), F32),
            VMEM((TRIPLES, COLS), F32),
            VMEM((TRIPLES, STEP), jnp.int32),
            VMEM((TRIPLES, STEP), jnp.int32),
            VMEM((2, 1024, COLS), BF16),
            VMEM((8, 8, STEP), F32),
            VMEM((2, TRIPLES, COLS), BF16),
            VMEM((8, TRIPLES, STEP), BF16),
            VMEM((2, TRIPLES, COLS), BF16),
            VMEM((2, TRIPLES, COLS), BF16),
            VMEM((2, 1024, COLS), F32),
            VMEM((1024, COLS), F32),
            VMEM((1024, COLS), F32),
            VMEM((3, 4, 4, 16, COLS), WIRE),
            VMEM((3, 4, 4, 16, COLS), WIRE),
            VMEM((4, 4, 16, COLS), F32),
            VMEM((3, 4, 16, COLS), WIRE),
            VMEM((3, 4, 16, COLS), WIRE),
            VMEM((4, 16, COLS), F32),
            VMEM((4, 2, 8, COLS), F32),
            VMEM((8, COLS), F32),
            VMEM((8, COLS), F32),
            VMEM((3, 4, 4, 16, COLS), WIRE),
            VMEM((3, 4, 4, 16, COLS), WIRE),
            VMEM((4, 4, 16, COLS), F32),
            VMEM((3, 4, 16, COLS), WIRE),
            VMEM((3, 4, 16, COLS), WIRE),
            VMEM((4, 16, COLS), F32),
            VMEM((4, 4, 16, COLS), WIRE),
        ],
        compiler_params=pltpu.CompilerParams(collective_id=0, has_side_effects=True, vmem_limit_bytes=36 << 20),
        name="step",
    )(*(pltpu.with_memory_space_constraint(v, pltpu.HBM) for v in (
        known_tails.T, head_owner.reshape(1, TRIPLES), head_row.reshape(1, TRIPLES), relation.reshape(1, TRIPLES),
        tail_ids.reshape(1, TRIPLES), phases, entity_table)))
    return e, r.astype(F32)


def solution(mesh):
    in_specs = (
        P("ent", None),
        P("rel", None),
        P(("ent", "rel"), None),
        P(("ent", "rel")),
        P(("ent", "rel")),
        P(("ent", "rel")),
        P(("ent", "rel"), None),
    )
    out_specs = (P(("ent", "rel"), None), P("rel", None))
    return jax.shard_map(local, mesh=mesh, in_specs=in_specs, out_specs=out_specs, check_vma=False)
```

```python
import functools

import jax
import jax.numpy as jnp
from jax import lax
from jax.experimental import pallas as pl
from jax.experimental.pallas import tpu as pltpu
from jax.sharding import PartitionSpec as P

MESH = pl.DeviceIdType.MESH
VMEM = pltpu.VMEM
F32 = jnp.float32
BF16 = jnp.bfloat16
WIRE = jnp.bfloat16
COLS = 512

SIN = (0.9999999999932018, -0.16666666657817392, 0.008333333144447052, -0.00019841254471923497,
       2.7556704311932283e-06, -2.5038717712098566e-08, 1.5896746642760318e-10, -6.610935072102146e-13)
COS = (0.9999999999990714, -0.4999999999846839, 0.041666666625163704, -0.0013888888455803566,
       2.480156464708791e-05, -2.755665269895137e-07, 2.0865211281170485e-09, -1.1353643820753535e-11,
       4.131574377242709e-14)


def horner(coefficients, t):
    value = jnp.full_like(t, coefficients[-1])
    for c in coefficients[-2::-1]:
        value = value * t + c
    return value


def place():
    e = lax.axis_index("ent")
    r = lax.axis_index("rel")
    return e // 16, (e // 4) % 4, e % 4, r // 2, r % 2


def device(x, y, zh, zl, core):
    return {"ent": x * 16 + y * 4 + zh, "rel": zl * 2 + core}


class Wire:
    def __init__(self, send, recv):
        self.send, self.recv = send, recv
        self.count = 0
        self.open = []

    def number(self):
        self.count += 1
        return self.count - 1

    def start(self, t, src, dst, to):
        copy = pltpu.make_async_remote_copy(
            src_ref=src, dst_ref=dst, send_sem=self.send.at[t], recv_sem=self.recv.at[t],
            device_id=to, device_id_type=MESH)
        copy.start()
        self.open.append(copy)

    def wait(self, t, dst, to):
        pltpu.make_async_remote_copy(
            src_ref=dst, dst_ref=dst, send_sem=self.send.at[t], recv_sem=self.recv.at[t],
            device_id=to, device_id_type=MESH).wait_recv()

    def drain(self):
        for copy in self.open:
            copy.wait_send()
        self.open = []


def greet(x, y, zh, zl, core):
    barrier = pltpu.get_barrier_semaphore()
    z = zh * 2 + zl
    peers = [device(x, y, zh, zl, 1 - core)]
    for d in (1, 2, 3):
        peers.append(device((x + d) % 4, y, zh, zl, core))
        peers.append(device(x, (y + d) % 4, zh, zl, core))
    for d in range(1, 8):
        zz = (z + d) % 8
        peers.append(device(x, y, zz // 2, zz % 2, core))
    for peer in peers:
        pl.semaphore_signal(barrier, inc=1, device_id=peer, device_id_type=MESH)
    return lambda: pl.semaphore_wait(barrier, len(peers))


class Spread:
    def __init__(self, wire, block, to, a0, b0, ks, z_to):
        self.w, self.block, self.to, self.a0, self.b0 = wire, block, to, a0, b0
        self.z_to, self.ks = z_to, ks
        self.tz = [wire.number() for _ in z_to]
        self.tb = [[wire.number() for _ in range(3)] for _ in range(4)]
        self.ta = [[[wire.number() for _ in range(3)] for _ in range(4)] for _ in range(4)]

    def along(self, q, j):
        blk = self.block(self.a0, (self.b0 + j) % 4, self.ks[q])
        for k in (2, 1, 3):
            self.w.start(self.ta[q][j][k - 1], blk, blk, self.to((self.a0 + k) % 4, self.b0))

    def on(self, q):
        blk = self.block(self.a0, self.b0, self.ks[q])
        for k in (2, 1, 3):
            self.w.start(self.tb[q][k - 1], blk, blk, self.to(self.a0, (self.b0 + k) % 4))
        self.along(q, 0)

    def begin(self):
        blk = self.block(self.a0, self.b0, self.ks[0])
        for i in range(3):
            self.w.start(self.tz[i], blk, blk, self.z_to[i])
        self.on(0)

    def take_z(self, i):
        self.w.wait(self.tz[i], self.block(self.a0, self.b0, self.ks[1 + i]), self.z_to[i])
        self.on(1 + i)

    def take_b(self, q):
        for k in (1, 3, 2):
            j = 4 - k
            b = (self.b0 + j) % 4
            self.w.wait(self.tb[q][k - 1], self.block(self.a0, b, self.ks[q]), self.to(self.a0, b))
            self.along(q, j)

    def take_a(self, q, j):
        for k in (1, 3, 2):
            a = (self.a0 + 4 - k) % 4
            self.w.wait(self.ta[q][j][k - 1], self.block(a, (self.b0 + j) % 4, self.ks[q]), self.to(a, self.b0))


FAR = (2, 1, 3, 0)


class Chain:
    def __init__(self, wire, load, to, a0, b0, ks, bufs):
        self.w, self.load, self.to, self.a0, self.b0 = wire, load, to, a0, b0
        self.ks = ks
        self.out_a, self.in_a, self.small, self.out_b, self.in_b, self.last = bufs
        self.ta = [[wire.number() for _ in range(3)] for _ in range(4)]
        self.tb = [[wire.number() for _ in range(3)] for _ in range(4)]

    def piece(self, c, q):
        return jnp.concatenate([self.load(c, b, self.ks[q])[None] for b in range(4)], axis=0)

    def begin_a(self, q):
        for k in (2, 1, 3):
            c = (self.a0 + k) % 4
            self.out_a[k - 1, q] = self.piece(c, q).astype(self.out_a.dtype)
            self.w.start(self.ta[q][k - 1], self.out_a.at[k - 1, q], self.in_a.at[k - 1, q], self.to(c, self.b0))

    def turn_b(self, q):
        for k in (1, 3, 2):
            self.w.wait(self.ta[q][k - 1], self.in_a.at[k - 1, q], self.to((self.a0 + 4 - k) % 4, self.b0))
        near = self.in_a[0, q].astype(F32) + self.in_a[2, q].astype(F32)
        self.small[q] = self.piece(self.a0, q) + (near + self.in_a[1, q].astype(F32))
        for k in (2, 1, 3):
            c = (self.b0 + k) % 4
            self.out_b[k - 1, q] = self.small[q, c].astype(self.out_b.dtype)
            self.w.start(self.tb[q][k - 1], self.out_b.at[k - 1, q], self.in_b.at[k - 1, q], self.to(self.a0, c))

    def end_b(self, q):
        for k in (1, 3, 2):
            self.w.wait(self.tb[q][k - 1], self.in_b.at[k - 1, q], self.to(self.a0, (self.b0 + 4 - k) % 4))
        near = self.in_b[0, q].astype(F32) + self.in_b[2, q].astype(F32)
        self.last[q] = self.small[q, self.b0] + (near + self.in_b[1, q].astype(F32))


def dot(a, b):
    return jnp.dot(a, b, preferred_element_type=F32)


def dot_nt(a, b):
    return lax.dot_general(a, b, (((1,), (1,)), ((), ())), preferred_element_type=F32)


def dot_tn(a, b):
    return lax.dot_general(a, b, (((0,), (0,)), ((), ())), preferred_element_type=F32)


def span(i, n):
    return pl.ds(pl.multiple_of(i * n, n), n)


STEP = 128
MAIN = 512
DENSE = 256
TRIPLES = 512
LISTED = 32


def step_kernel(known_hbm, owner_hbm, place_hbm, relation_hbm, tail_hbm, phases_hbm, entity_hbm, e_ref, r_ref,
                send, recv, local_sem,
                known_ref, owner_ref, place_ref, relation_ref, tail_ref, phases_ref, parts, cos_ref, sin_ref, word_ref, hot_ref, head_ref, table_ref, square_ref,
                query_ref, weight_ref, back_ref, turn_ref, g_ref, pair, d_ref,
                ga_out, ga_in, g_small, gb_out, gb_in, g_sum, g_zin, g_last, g_swap,
                da_out, da_in, d_small, db_out, db_in, d_sum, d_zin):
    x, y, zh, zl, core = place()
    other = 1 - core
    z_sign = 2 * zl - 1
    mine = span(core, COLS)
    theirs = span(other, COLS)
    partner = device(x, y, zh, zl, other)
    w = Wire(send, recv)

    ga, gb = x * other + y * core, y * other + x * core
    da, db = gb, ga

    def gxy(a, b):
        return a * other + b * core, b * other + a * core

    def dxy(a, b):
        return b * other + a * core, a * other + b * core

    def gspan(a, b):
        px, py = gxy(a, b)
        return span(px * 4 + py, 64)

    def dspan(a, b):
        px, py = dxy(a, b)
        return span(px * 4 + py, 64)

    def gto(a, b):
        px, py = gxy(a, b)
        return device(px, py, zh, zl, core)

    def dto(a, b):
        px, py = dxy(a, b)
        return device(px, py, zh, zl, core)

    everyone = greet(x, y, zh, zl, core)

    tp = [w.number() for _ in range(16)]

    def block(a, b, k):
        px, py = gxy(a, b)
        return table_ref.at[core, span((px * 4 + py) * 4 + k, 16)]

    z_to = [device(x, y, (zh + z_sign + 4) % 4, 1 - zl, core), device(x, y, (zh + z_sign + 4) % 4, zl, core),
            device(x, y, (zh + 2) % 4, 1 - zl, core)]
    z_from = [(zh + z_sign + 4) % 4, (zh - z_sign + 4) % 4, (zh + 2) % 4]
    own = pltpu.make_async_copy(entity_hbm.at[:, mine], block(ga, gb, zh), local_sem.at[0])
    own.start()
    pairs = ((phases_hbm, phases_ref), (known_hbm, known_ref), (owner_hbm, owner_ref), (place_hbm, place_ref),
             (relation_hbm, relation_ref), (tail_hbm, tail_ref))
    fetches = [pltpu.make_async_copy(a, b, local_sem.at[1 + i]) for i, (a, b) in enumerate(pairs)]
    for f in fetches:
        f.start()
    own.wait()
    everyone()
    spread = Spread(w, block, gto, ga, gb, [zh] + z_from, z_to)
    spread.begin()

    def push(i, a, b):
        part = table_ref.at[core, gspan(a, b)]
        w.start(tp[i], part, part, partner)

    for f in fetches:
        f.wait()

    def split(i, _):
        at = span(i, STEP)
        p = phases_ref[at]
        for k in range(3):
            q = p.astype(BF16)
            parts[k, at] = q
            p = p - q.astype(F32)
        return 0

    lax.fori_loop(0, 8, split, 0)

    lane = lax.broadcasted_iota(jnp.int32, (1, STEP), 1)

    def down(row):
        return jnp.transpose(jnp.broadcast_to(row, (STEP, STEP)))

    def hot_rows(col):
        return jnp.concatenate([(col == lane + 128 * k).astype(F32).astype(BF16) for k in range(8)], axis=1)

    def prepare(i, _):
        at = span(i, STEP)
        hot_ref[at] = hot_rows(down(owner_ref[:, at] * 4 + place_ref[:, at]))
        hot = hot_rows(down(relation_ref[:, at]))
        angle = dot(hot, parts[0]) + dot(hot, parts[1]) + dot(hot, parts[2])
        t = angle * angle
        cos_ref[at] = horner(COS, t)
        sin_ref[at] = angle * horner(SIN, t)
        ids = jnp.transpose(known_ref[:, at])
        low = ids & 127
        bit = jnp.left_shift(jnp.int32(1), jnp.right_shift(ids, 7))
        word = jnp.zeros((STEP, STEP), jnp.int32)
        for j in range(LISTED):
            word = word | jnp.where(low[:, j:j + 1] == lane, bit[:, j:j + 1], 0)
        tail = down(tail_ref[:, at])
        keep = jnp.where((tail & 127) == lane, jnp.left_shift(jnp.int32(1), jnp.right_shift(tail, 7)), 0)
        word_ref[at] = (word & ~keep) | jnp.left_shift(keep, 8)
        return 0

    spread.take_z(0)
    spread.take_b(0)
    lax.fori_loop(0, 1, prepare, 0)
    spread.take_z(1)
    spread.take_z(2)
    lax.fori_loop(1, 2, prepare, 0)
    for q in (1, 2, 3):
        spread.take_b(q)
    for j in range(4):
        push(j, ga, (gb + j) % 4)
    lax.fori_loop(2, 4, prepare, 0)
    for j in (0, 3, 1, 2):
        for q in range(4):
            spread.take_a(q, j)
        for k in (1, 3, 2):
            push(4 * k + j, (ga + 4 - k) % 4, (gb + j) % 4)
    def squares(c, i):
        t = table_ref[c, span(i, STEP)].astype(F32)
        s = jnp.sum(t * t, axis=1, keepdims=True)
        return jnp.transpose(jnp.broadcast_to(s, (STEP, STEP)))[0:8]

    def half_first(i, _):
        square_ref[i] = squares(core, i)
        return 0

    def half_second(i, _):
        square_ref[i] = square_ref[i] + squares(other, i)
        return 0

    lax.fori_loop(0, 8, half_first, 0)
    head_ref[core] = dot(hot_ref[...], table_ref[core])
    for i in range(16):
        w.wait(tp[i], table_ref.at[other, pl.ds(0, 64)], partner)

    lax.fori_loop(0, 8, half_second, 0)
    head_ref[other] = dot(hot_ref[...], table_ref[other])

    def main(i, _):
        at = span(i, MAIN)
        c, s = cos_ref[at], sin_ref[at]
        hr, hm = head_ref[0, at], head_ref[1, at]
        qr = hr * c - hm * s
        qm = hr * s + hm * c
        query_r, query_m = qr.astype(BF16), qm.astype(BF16)
        query_ref[0, at] = query_r
        query_ref[1, at] = query_m
        near_r, near_m = query_r.astype(F32), query_m.astype(F32)
        query_sq = jnp.sum(near_r * near_r + near_m * near_m, axis=1, keepdims=True)
        cross = dot_nt(query_r, table_ref[0]) + dot_nt(query_m, table_ref[1])
        word = word_ref[at]
        scores, hidden = [], []
        top = None
        for k in range(8):
            sc = 2.0 * cross[:, k * 128:(k + 1) * 128] - query_sq - square_ref[k, 0:1]
            hide = (word & (1 << k)) != 0
            scores.append(sc)
            hidden.append(hide)
            seen = jnp.where(hide, -jnp.inf, sc)
            top = seen if top is None else jnp.maximum(top, seen)
        top = jnp.max(top, axis=1, keepdims=True)
        raws = []
        for k in range(8):
            raws.append(jnp.where(hidden[k], 0.0, jnp.exp(scores[k] - top)))
        total = raws[0]
        for k in range(1, 8):
            total = total + raws[k]
        scale = 2.0 / jnp.sum(total, axis=1, keepdims=True)
        weights = []
        for k in range(8):
            hit = (word & (256 << k)) != 0
            wk = (raws[k] * scale - jnp.where(hit, 2.0, 0.0)).astype(BF16)
            weights.append(wk)
            weight_ref[k, at] = wk
        both = jnp.concatenate(weights, axis=1)
        gr, gm = dot(both, table_ref[0]), dot(both, table_ref[1])
        back_ref[0, at] = (gr * c + gm * s).astype(BF16)
        back_ref[1, at] = (gm * c - gr * s).astype(BF16)
        turn = qr * gm - qm * gr
        high = turn.astype(BF16)
        turn_ref[0, at] = high
        turn_ref[1, at] = (turn - high.astype(F32)).astype(BF16)
        return 0

    lax.fori_loop(0, TRIPLES // MAIN, main, 0)

    def key(i):
        return lax.broadcasted_iota(jnp.int32, (DENSE, 1), 0) + i * DENSE

    def relations(i, _):
        hot = (relation_ref[...] == key(i)).astype(F32).astype(BF16)
        d_ref[span(i, DENSE)] = dot(hot, turn_ref[0]) + dot(hot, turn_ref[1])
        return 0

    lax.fori_loop(0, 1024 // DENSE, relations, 0)

    def d_load(a, b, k):
        px, py = dxy(a, b)
        return d_ref[span((px * 4 + py) * 4 + k, 16)]

    d_chain = Chain(w, d_load, dto, da, db, list(range(4)), (da_out, da_in, d_small, db_out, db_in, d_sum))
    for q in range(4):
        d_chain.begin_a(q)

    ones = jnp.ones((TRIPLES, 128), BF16)
    heads = owner_ref[...] * 4 + place_ref[...]

    def dense(i):
        at = span(i, DENSE)
        wk = jnp.concatenate([weight_ref[i * (DENSE // 128) + k] for k in range(DENSE // 128)], axis=1)
        counts = dot_tn(wk, ones)
        hot = (heads == key(i)).astype(F32).astype(BF16)
        many = jnp.concatenate([counts] * 4, axis=1)
        for c in range(2):
            sums = dot_tn(wk, query_ref[c]) + dot(hot, back_ref[c])
            g_ref[c, at] = sums - many * table_ref[c, at].astype(F32)

    tg = [w.number() for _ in range(4)]

    def dense_of(n):
        i = (x + 2 + n) % 4
        dense(i)
        w.start(tg[n], g_ref.at[other, span(i, DENSE)], pair.at[span(i, DENSE)], partner)

    tdz = [[w.number() for _ in range(3)] for _ in range(4)]

    def share(q):
        d_chain.end_b(q)
        d_zin[zh, q] = d_sum[q].astype(d_zin.dtype)
        for k in (2, 1, 3):
            to = device(x, y, (zh + k) % 4, zl, core)
            w.start(tdz[q][k - 1], d_zin.at[zh, q], d_zin.at[zh, q], to)

    def r_block(a, b, k):
        px, py = dxy(a, b)
        return r_ref.at[span((px * 4 + py) * 4 + k, 16)]

    back = Spread(w, r_block, dto, da, db, list(range(4)), [])

    def settle(q):
        for k in (1, 3, 2):
            w.wait(tdz[q][k - 1], d_zin.at[(zh + 4 - k) % 4, q], partner)
        z = [d_zin[k, q].astype(F32) for k in range(4)]
        r_block(da, db, q)[...] = ((z[0] + z[1]) + (z[2] + z[3])).astype(r_ref.dtype)
        back.on(q)

    def g_load(a, b, k):
        px, py = gxy(a, b)
        at = span((px * 4 + py) * 4 + k, 16)
        return g_ref[core, at] + pair[at]

    g_chain = Chain(w, g_load, gto, ga, gb, [(zh + off) % 4 for off in FAR],
                    (ga_out, ga_in, g_small, gb_out, gb_in, g_sum))
    tgz = [[w.number() for _ in range(2)] for _ in range(4)]
    here = [(FAR.index(off), off, dl) for off in FAR for dl in range(2)]
    here = [(q, off, dl) for q, off, dl in here if off or dl]

    def end_g(q):
        g_chain.end_b(q)
        for qq, off, dl in here:
            if qq == q:
                ll = (zl + dl) % 2
                w.start(tgz[off][dl], g_sum.at[q, span(ll, 8)], g_zin.at[off, dl], device(x, y, (zh + off) % 4, ll, core))

    ts = w.number()

    def pairs_in():
        for n in range(4):
            w.wait(tg[n], pair.at[span((x + 2 + n) % 4, DENSE)], partner)

    def send_last():
        total = g_sum[3, span(zl, 8)]
        for q, off, dl in here:
            w.wait(tgz[off][dl], g_zin.at[off, dl], partner)
            total = total + g_zin[off, dl]
        g_last[...] = total
        w.start(ts, g_last, g_swap, partner)

    def finish():
        w.wait(ts, g_swap, partner)
        first, second = g_last[...], g_swap[...]
        left = jnp.where(core == 0, first, second)
        right = jnp.where(core == 0, second, first)
        e_ref[:, 0:COLS] = jnp.where(core == 0, left[0:4], left[4:8])
        e_ref[:, COLS:2 * COLS] = jnp.where(core == 0, right[0:4], right[4:8])

    def ahead(j):
        for q in range(4):
            back.take_a(q, j)

    dense_of(0)
    dense_of(1)
    dense_of(2)
    dense_of(3)
    d_chain.turn_b(0)
    d_chain.turn_b(1)
    pairs_in()
    g_chain.begin_a(0)
    g_chain.begin_a(1)
    d_chain.turn_b(2)
    d_chain.turn_b(3)
    g_chain.begin_a(2)
    g_chain.begin_a(3)
    share(0)
    share(1)
    share(2)
    share(3)
    g_chain.turn_b(0)
    g_chain.turn_b(1)
    g_chain.turn_b(2)
    g_chain.turn_b(3)
    settle(0)
    settle(1)
    settle(2)
    settle(3)
    back.take_b(0)
    end_g(0)
    back.take_b(1)
    end_g(1)
    back.take_b(2)
    end_g(2)
    back.take_b(3)
    end_g(3)
    send_last()
    finish()
    ahead(0)
    ahead(3)
    ahead(1)
    ahead(2)
    w.drain()


def local(entity_table, phases, head_owner, head_row, relation, tail_ids, known_tails):
    messages = 16 + 63 + 24 + 4 + 24 + 12 + 60 + 8 + 1
    here = pl.BlockSpec(memory_space=VMEM)
    e, r = pl.pallas_call(
        step_kernel,
        out_shape=(jax.ShapeDtypeStruct((4, 2 * COLS), F32), jax.ShapeDtypeStruct((1024, COLS), WIRE)),
        in_specs=[pl.BlockSpec(memory_space=pltpu.HBM)] * 7,
        out_specs=[here, here],
        scratch_shapes=[
            pltpu.SemaphoreType.DMA((messages,)),
            pltpu.SemaphoreType.DMA((messages,)),
            pltpu.SemaphoreType.DMA((7,)),
            VMEM((LISTED, TRIPLES), jnp.int32),
            VMEM((1, TRIPLES), jnp.int32),
            VMEM((1, TRIPLES), jnp.int32),
            VMEM((1, TRIPLES), jnp.int32),
            VMEM((1, TRIPLES), jnp.int32),
            VMEM((1024, COLS), F32),
            VMEM((3, 1024, COLS), BF16),
            VMEM((TRIPLES, COLS), F32),
            VMEM((TRIPLES, COLS), F32),
            VMEM((TRIPLES, STEP), jnp.int32),
            VMEM((TRIPLES, 1024), BF16),
            VMEM((2, TRIPLES, COLS), F32),
            VMEM((2, 1024, COLS), BF16),
            VMEM((8, 8, STEP), F32),
            VMEM((2, TRIPLES, COLS), BF16),
            VMEM((8, TRIPLES, STEP), BF16),
            VMEM((2, TRIPLES, COLS), BF16),
            VMEM((2, TRIPLES, COLS), BF16),
            VMEM((2, 1024, COLS), F32),
            VMEM((1024, COLS), F32),
            VMEM((1024, COLS), F32),
            VMEM((3, 4, 4, 16, COLS), WIRE),
            VMEM((3, 4, 4, 16, COLS), WIRE),
            VMEM((4, 4, 16, COLS), F32),
            VMEM((3, 4, 16, COLS), WIRE),
            VMEM((3, 4, 16, COLS), WIRE),
            VMEM((4, 16, COLS), F32),
            VMEM((4, 2, 8, COLS), F32),
            VMEM((8, COLS), F32),
            VMEM((8, COLS), F32),
            VMEM((3, 4, 4, 16, COLS), WIRE),
            VMEM((3, 4, 4, 16, COLS), WIRE),
            VMEM((4, 4, 16, COLS), F32),
            VMEM((3, 4, 16, COLS), WIRE),
            VMEM((3, 4, 16, COLS), WIRE),
            VMEM((4, 16, COLS), F32),
            VMEM((4, 4, 16, COLS), WIRE),
        ],
        compiler_params=pltpu.CompilerParams(collective_id=0, has_side_effects=True, vmem_limit_bytes=42 << 20),
        name="step",
    )(*(pltpu.with_memory_space_constraint(v, pltpu.HBM) for v in (
        known_tails.T, head_owner.reshape(1, TRIPLES), head_row.reshape(1, TRIPLES), relation.reshape(1, TRIPLES),
        tail_ids.reshape(1, TRIPLES), phases, entity_table)))
    return e, r.astype(F32)


def solution(mesh):
    in_specs = (
        P("ent", None),
        P("rel", None),
        P(("ent", "rel"), None),
        P(("ent", "rel")),
        P(("ent", "rel")),
        P(("ent", "rel")),
        P(("ent", "rel"), None),
    )
    out_specs = (P(("ent", "rel"), None), P("rel", None))
    return jax.shard_map(local, mesh=mesh, in_specs=in_specs, out_specs=out_specs, check_vma=False)
```

```python
import functools

import jax
import jax.numpy as jnp
from jax import lax
from jax.experimental import pallas as pl
from jax.experimental.pallas import tpu as pltpu
from jax.sharding import PartitionSpec as P

MESH = pl.DeviceIdType.MESH
VMEM = pltpu.VMEM
F32 = jnp.float32
BF16 = jnp.bfloat16
WIRE = jnp.bfloat16
COLS = 512

SIN = (0.9999999999932018, -0.16666666657817392, 0.008333333144447052, -0.00019841254471923497,
       2.7556704311932283e-06, -2.5038717712098566e-08, 1.5896746642760318e-10, -6.610935072102146e-13)
COS = (0.9999999999990714, -0.4999999999846839, 0.041666666625163704, -0.0013888888455803566,
       2.480156464708791e-05, -2.755665269895137e-07, 2.0865211281170485e-09, -1.1353643820753535e-11,
       4.131574377242709e-14)


def horner(coefficients, t):
    value = jnp.full_like(t, coefficients[-1])
    for c in coefficients[-2::-1]:
        value = value * t + c
    return value


def place():
    e = lax.axis_index("ent")
    r = lax.axis_index("rel")
    return e // 16, (e // 4) % 4, e % 4, r // 2, r % 2


def device(x, y, zh, zl, core):
    return {"ent": x * 16 + y * 4 + zh, "rel": zl * 2 + core}


class Wire:
    def __init__(self, send, recv):
        self.send, self.recv = send, recv
        self.count = 0
        self.open = []

    def number(self):
        self.count += 1
        return self.count - 1

    def start(self, t, src, dst, to):
        copy = pltpu.make_async_remote_copy(
            src_ref=src, dst_ref=dst, send_sem=self.send.at[t], recv_sem=self.recv.at[t],
            device_id=to, device_id_type=MESH)
        copy.start()
        self.open.append(copy)

    def wait(self, t, dst, to):
        pltpu.make_async_remote_copy(
            src_ref=dst, dst_ref=dst, send_sem=self.send.at[t], recv_sem=self.recv.at[t],
            device_id=to, device_id_type=MESH).wait_recv()

    def drain(self):
        for copy in self.open:
            copy.wait_send()
        self.open = []


def greet(x, y, zh, zl, core):
    barrier = pltpu.get_barrier_semaphore()
    z = zh * 2 + zl
    peers = [device(x, y, zh, zl, 1 - core)]
    for d in (1, 2, 3):
        peers.append(device((x + d) % 4, y, zh, zl, core))
        peers.append(device(x, (y + d) % 4, zh, zl, core))
    for d in range(1, 8):
        zz = (z + d) % 8
        peers.append(device(x, y, zz // 2, zz % 2, core))
    for peer in peers:
        pl.semaphore_signal(barrier, inc=1, device_id=peer, device_id_type=MESH)
    return lambda: pl.semaphore_wait(barrier, len(peers))


class Spread:
    def __init__(self, wire, block, to, a0, b0, ks, z_to):
        self.w, self.block, self.to, self.a0, self.b0 = wire, block, to, a0, b0
        self.z_to, self.ks = z_to, ks
        self.tz = [wire.number() for _ in z_to]
        self.tb = [[wire.number() for _ in range(3)] for _ in range(4)]
        self.ta = [[[wire.number() for _ in range(3)] for _ in range(4)] for _ in range(4)]

    def along(self, q, j):
        blk = self.block(self.a0, (self.b0 + j) % 4, self.ks[q])
        for k in (2, 1, 3):
            self.w.start(self.ta[q][j][k - 1], blk, blk, self.to((self.a0 + k) % 4, self.b0))

    def on(self, q):
        blk = self.block(self.a0, self.b0, self.ks[q])
        for k in (2, 1, 3):
            self.w.start(self.tb[q][k - 1], blk, blk, self.to(self.a0, (self.b0 + k) % 4))
        self.along(q, 0)

    def begin(self):
        blk = self.block(self.a0, self.b0, self.ks[0])
        for i in range(3):
            self.w.start(self.tz[i], blk, blk, self.z_to[i])
        self.on(0)

    def take_z(self, i):
        self.w.wait(self.tz[i], self.block(self.a0, self.b0, self.ks[1 + i]), self.z_to[i])
        self.on(1 + i)

    def take_b(self, q):
        for k in (1, 3, 2):
            j = 4 - k
            b = (self.b0 + j) % 4
            self.w.wait(self.tb[q][k - 1], self.block(self.a0, b, self.ks[q]), self.to(self.a0, b))
            self.along(q, j)

    def take_a(self, q, j):
        for k in (1, 3, 2):
            a = (self.a0 + 4 - k) % 4
            self.w.wait(self.ta[q][j][k - 1], self.block(a, (self.b0 + j) % 4, self.ks[q]), self.to(a, self.b0))


FAR = (2, 1, 3, 0)


class Chain:
    def __init__(self, wire, load, to, a0, b0, ks, bufs):
        self.w, self.load, self.to, self.a0, self.b0 = wire, load, to, a0, b0
        self.ks = ks
        self.out_a, self.in_a, self.small, self.out_b, self.in_b, self.last = bufs
        self.ta = [[wire.number() for _ in range(3)] for _ in range(4)]
        self.tb = [[wire.number() for _ in range(3)] for _ in range(4)]

    def piece(self, c, q):
        return jnp.concatenate([self.load(c, b, self.ks[q])[None] for b in range(4)], axis=0)

    def begin_a(self, q):
        for k in (2, 1, 3):
            c = (self.a0 + k) % 4
            self.out_a[k - 1, q] = self.piece(c, q).astype(self.out_a.dtype)
            self.w.start(self.ta[q][k - 1], self.out_a.at[k - 1, q], self.in_a.at[k - 1, q], self.to(c, self.b0))

    def turn_b(self, q):
        for k in (1, 3, 2):
            self.w.wait(self.ta[q][k - 1], self.in_a.at[k - 1, q], self.to((self.a0 + 4 - k) % 4, self.b0))
        near = self.in_a[0, q].astype(F32) + self.in_a[2, q].astype(F32)
        self.small[q] = self.piece(self.a0, q) + (near + self.in_a[1, q].astype(F32))
        for k in (2, 1, 3):
            c = (self.b0 + k) % 4
            self.out_b[k - 1, q] = self.small[q, c].astype(self.out_b.dtype)
            self.w.start(self.tb[q][k - 1], self.out_b.at[k - 1, q], self.in_b.at[k - 1, q], self.to(self.a0, c))

    def end_b(self, q):
        for k in (1, 3, 2):
            self.w.wait(self.tb[q][k - 1], self.in_b.at[k - 1, q], self.to(self.a0, (self.b0 + 4 - k) % 4))
        near = self.in_b[0, q].astype(F32) + self.in_b[2, q].astype(F32)
        self.last[q] = self.small[q, self.b0] + (near + self.in_b[1, q].astype(F32))


def dot(a, b):
    return jnp.dot(a, b, preferred_element_type=F32)


def dot_nt(a, b):
    return lax.dot_general(a, b, (((1,), (1,)), ((), ())), preferred_element_type=F32)


def dot_tn(a, b):
    return lax.dot_general(a, b, (((0,), (0,)), ((), ())), preferred_element_type=F32)


def span(i, n):
    return pl.ds(pl.multiple_of(i * n, n), n)


STEP = 128
MAIN = 512
DENSE = 256
TRIPLES = 512
LISTED = 32


def step_kernel(known_hbm, owner_hbm, place_hbm, relation_hbm, tail_hbm, phases_hbm, entity_hbm, e_ref, r_ref,
                send, recv, local_sem,
                known_ref, owner_ref, place_ref, relation_ref, tail_ref, phases_ref, parts, cos_ref, sin_ref, word_ref, head_ref, table_ref, square_ref,
                query_ref, weight_ref, back_ref, turn_ref, g_ref, pair, d_ref,
                ga_out, ga_in, g_small, gb_out, gb_in, g_sum, g_zin, g_last, g_swap,
                da_out, da_in, d_small, db_out, db_in, d_sum, d_zin):
    x, y, zh, zl, core = place()
    other = 1 - core
    z_sign = 2 * zl - 1
    mine = span(core, COLS)
    theirs = span(other, COLS)
    partner = device(x, y, zh, zl, other)
    w = Wire(send, recv)

    ga, gb = x * other + y * core, y * other + x * core
    da, db = gb, ga

    def gxy(a, b):
        return a * other + b * core, b * other + a * core

    def dxy(a, b):
        return b * other + a * core, a * other + b * core

    def gspan(a, b):
        px, py = gxy(a, b)
        return span(px * 4 + py, 64)

    def dspan(a, b):
        px, py = dxy(a, b)
        return span(px * 4 + py, 64)

    def gto(a, b):
        px, py = gxy(a, b)
        return device(px, py, zh, zl, core)

    def dto(a, b):
        px, py = dxy(a, b)
        return device(px, py, zh, zl, core)

    everyone = greet(x, y, zh, zl, core)

    tp = [w.number() for _ in range(16)]

    def block(a, b, k):
        px, py = gxy(a, b)
        return table_ref.at[core, span((px * 4 + py) * 4 + k, 16)]

    z_to = [device(x, y, (zh + z_sign + 4) % 4, 1 - zl, core), device(x, y, (zh + z_sign + 4) % 4, zl, core),
            device(x, y, (zh + 2) % 4, 1 - zl, core)]
    z_from = [(zh + z_sign + 4) % 4, (zh - z_sign + 4) % 4, (zh + 2) % 4]
    own = pltpu.make_async_copy(entity_hbm.at[:, mine], block(ga, gb, zh), local_sem.at[0])
    own.start()
    pairs = ((phases_hbm, phases_ref), (known_hbm, known_ref), (owner_hbm, owner_ref), (place_hbm, place_ref),
             (relation_hbm, relation_ref), (tail_hbm, tail_ref))
    fetches = [pltpu.make_async_copy(a, b, local_sem.at[1 + i]) for i, (a, b) in enumerate(pairs)]
    for f in fetches:
        f.start()
    own.wait()
    everyone()
    spread = Spread(w, block, gto, ga, gb, [zh] + z_from, z_to)
    spread.begin()

    def push(i, a, b):
        part = table_ref.at[core, gspan(a, b)]
        w.start(tp[i], part, part, partner)

    for f in fetches:
        f.wait()

    def split(i, _):
        at = span(i, STEP)
        p = phases_ref[at]
        for k in range(3):
            q = p.astype(BF16)
            parts[k, at] = q
            p = p - q.astype(F32)
        return 0

    lax.fori_loop(0, 8, split, 0)

    lane = lax.broadcasted_iota(jnp.int32, (1, STEP), 1)

    def down(row):
        return jnp.transpose(jnp.broadcast_to(row, (STEP, STEP)))

    def hot_rows(col):
        return jnp.concatenate([(col == lane + 128 * k).astype(F32).astype(BF16) for k in range(8)], axis=1)

    def prepare(i, _):
        at = span(i, STEP)
        head_ref[at] = hot_rows(down(owner_ref[:, at] * 4 + place_ref[:, at]))
        hot = hot_rows(down(relation_ref[:, at]))
        angle = dot(hot, parts[0]) + dot(hot, parts[1]) + dot(hot, parts[2])
        t = angle * angle
        cos_ref[at] = horner(COS, t)
        sin_ref[at] = angle * horner(SIN, t)
        ids = jnp.transpose(known_ref[:, at])
        low = ids & 127
        bit = jnp.left_shift(jnp.int32(1), jnp.right_shift(ids, 7))
        word = jnp.zeros((STEP, STEP), jnp.int32)
        for j in range(LISTED):
            word = word | jnp.where(low[:, j:j + 1] == lane, bit[:, j:j + 1], 0)
        tail = down(tail_ref[:, at])
        keep = jnp.where((tail & 127) == lane, jnp.left_shift(jnp.int32(1), jnp.right_shift(tail, 7)), 0)
        word_ref[at] = (word & ~keep) | jnp.left_shift(keep, 8)
        return 0

    spread.take_z(0)
    spread.take_b(0)
    lax.fori_loop(0, 1, prepare, 0)
    spread.take_z(1)
    spread.take_z(2)
    lax.fori_loop(1, 2, prepare, 0)
    for q in (1, 2, 3):
        spread.take_b(q)
    for j in range(4):
        push(j, ga, (gb + j) % 4)
    lax.fori_loop(2, 4, prepare, 0)
    for j in (0, 3, 1, 2):
        for q in range(4):
            spread.take_a(q, j)
        for k in (1, 3, 2):
            push(4 * k + j, (ga + 4 - k) % 4, (gb + j) % 4)
    for i in range(16):
        w.wait(tp[i], table_ref.at[other, pl.ds(0, 64)], partner)

    def squares(i, _):
        re, im = table_ref[0, span(i, STEP)].astype(F32), table_ref[1, span(i, STEP)].astype(F32)
        s = jnp.sum(re * re + im * im, axis=1, keepdims=True)
        square_ref[i] = jnp.transpose(jnp.broadcast_to(s, (STEP, STEP)))[0:8]
        return 0

    lax.fori_loop(0, 8, squares, 0)

    def main(i, _):
        at = span(i, MAIN)
        hot = head_ref[at]
        c, s = cos_ref[at], sin_ref[at]
        hr, hm = dot(hot, table_ref[0]), dot(hot, table_ref[1])
        qr = hr * c - hm * s
        qm = hr * s + hm * c
        query_r, query_m = qr.astype(BF16), qm.astype(BF16)
        query_ref[0, at] = query_r
        query_ref[1, at] = query_m
        near_r, near_m = query_r.astype(F32), query_m.astype(F32)
        query_sq = jnp.sum(near_r * near_r + near_m * near_m, axis=1, keepdims=True)
        cross = dot_nt(query_r, table_ref[0]) + dot_nt(query_m, table_ref[1])
        word = word_ref[at]
        scores, hidden = [], []
        top = None
        for k in range(8):
            sc = 2.0 * cross[:, k * 128:(k + 1) * 128] - query_sq - square_ref[k, 0:1]
            hide = (word & (1 << k)) != 0
            scores.append(sc)
            hidden.append(hide)
            seen = jnp.where(hide, -jnp.inf, sc)
            top = seen if top is None else jnp.maximum(top, seen)
        top = jnp.max(top, axis=1, keepdims=True)
        raws = []
        for k in range(8):
            raws.append(jnp.where(hidden[k], 0.0, jnp.exp(scores[k] - top)))
        total = raws[0]
        for k in range(1, 8):
            total = total + raws[k]
        scale = 2.0 / jnp.sum(total, axis=1, keepdims=True)
        weights = []
        for k in range(8):
            hit = (word & (256 << k)) != 0
            wk = (raws[k] * scale - jnp.where(hit, 2.0, 0.0)).astype(BF16)
            weights.append(wk)
            weight_ref[k, at] = wk
        both = jnp.concatenate(weights, axis=1)
        gr, gm = dot(both, table_ref[0]), dot(both, table_ref[1])
        back_ref[0, at] = (gr * c + gm * s).astype(BF16)
        back_ref[1, at] = (gm * c - gr * s).astype(BF16)
        turn = qr * gm - qm * gr
        high = turn.astype(BF16)
        turn_ref[0, at] = high
        turn_ref[1, at] = (turn - high.astype(F32)).astype(BF16)
        return 0

    lax.fori_loop(0, TRIPLES // MAIN, main, 0)

    def key(i):
        return lax.broadcasted_iota(jnp.int32, (DENSE, 1), 0) + i * DENSE

    def relations(i, _):
        hot = (relation_ref[...] == key(i)).astype(F32).astype(BF16)
        d_ref[span(i, DENSE)] = dot(hot, turn_ref[0]) + dot(hot, turn_ref[1])
        return 0

    lax.fori_loop(0, 1024 // DENSE, relations, 0)

    def d_load(a, b, k):
        px, py = dxy(a, b)
        return d_ref[span((px * 4 + py) * 4 + k, 16)]

    d_chain = Chain(w, d_load, dto, da, db, list(range(4)), (da_out, da_in, d_small, db_out, db_in, d_sum))
    for q in range(4):
        d_chain.begin_a(q)

    ones = jnp.ones((TRIPLES, 128), BF16)
    heads = owner_ref[...] * 4 + place_ref[...]

    def dense(i):
        at = span(i, DENSE)
        wk = jnp.concatenate([weight_ref[i * (DENSE // 128) + k] for k in range(DENSE // 128)], axis=1)
        counts = dot_tn(wk, ones)
        hot = (heads == key(i)).astype(F32).astype(BF16)
        many = jnp.concatenate([counts] * 4, axis=1)
        for c in range(2):
            sums = dot_tn(wk, query_ref[c]) + dot(hot, back_ref[c])
            g_ref[c, at] = sums - many * table_ref[c, at].astype(F32)

    tg = [w.number() for _ in range(4)]

    def dense_of(n):
        i = (x + 2 + n) % 4
        dense(i)
        w.start(tg[n], g_ref.at[other, span(i, DENSE)], pair.at[span(i, DENSE)], partner)

    tdz = [[w.number() for _ in range(3)] for _ in range(4)]

    def share(q):
        d_chain.end_b(q)
        d_zin[zh, q] = d_sum[q].astype(d_zin.dtype)
        for k in (2, 1, 3):
            to = device(x, y, (zh + k) % 4, zl, core)
            w.start(tdz[q][k - 1], d_zin.at[zh, q], d_zin.at[zh, q], to)

    def r_block(a, b, k):
        px, py = dxy(a, b)
        return r_ref.at[span((px * 4 + py) * 4 + k, 16)]

    back = Spread(w, r_block, dto, da, db, list(range(4)), [])

    def settle(q):
        for k in (1, 3, 2):
            w.wait(tdz[q][k - 1], d_zin.at[(zh + 4 - k) % 4, q], partner)
        z = [d_zin[k, q].astype(F32) for k in range(4)]
        r_block(da, db, q)[...] = ((z[0] + z[1]) + (z[2] + z[3])).astype(r_ref.dtype)
        back.on(q)

    def g_load(a, b, k):
        px, py = gxy(a, b)
        at = span((px * 4 + py) * 4 + k, 16)
        return g_ref[core, at] + pair[at]

    g_chain = Chain(w, g_load, gto, ga, gb, [(zh + off) % 4 for off in FAR],
                    (ga_out, ga_in, g_small, gb_out, gb_in, g_sum))
    tgz = [[w.number() for _ in range(2)] for _ in range(4)]
    here = [(FAR.index(off), off, dl) for off in FAR for dl in range(2)]
    here = [(q, off, dl) for q, off, dl in here if off or dl]

    def end_g(q):
        g_chain.end_b(q)
        for qq, off, dl in here:
            if qq == q:
                ll = (zl + dl) % 2
                w.start(tgz[off][dl], g_sum.at[q, span(ll, 8)], g_zin.at[off, dl], device(x, y, (zh + off) % 4, ll, core))

    ts = w.number()

    def pairs_in():
        for n in range(4):
            w.wait(tg[n], pair.at[span((x + 2 + n) % 4, DENSE)], partner)

    def send_last():
        total = g_sum[3, span(zl, 8)]
        for q, off, dl in here:
            w.wait(tgz[off][dl], g_zin.at[off, dl], partner)
            total = total + g_zin[off, dl]
        g_last[...] = total
        w.start(ts, g_last, g_swap, partner)

    def finish():
        w.wait(ts, g_swap, partner)
        first, second = g_last[...], g_swap[...]
        left = jnp.where(core == 0, first, second)
        right = jnp.where(core == 0, second, first)
        e_ref[:, 0:COLS] = jnp.where(core == 0, left[0:4], left[4:8])
        e_ref[:, COLS:2 * COLS] = jnp.where(core == 0, right[0:4], right[4:8])

    def ahead(j):
        for q in range(4):
            back.take_a(q, j)

    dense_of(0)
    dense_of(1)
    dense_of(2)
    dense_of(3)
    d_chain.turn_b(0)
    d_chain.turn_b(1)
    pairs_in()
    g_chain.begin_a(0)
    g_chain.begin_a(1)
    d_chain.turn_b(2)
    d_chain.turn_b(3)
    g_chain.begin_a(2)
    g_chain.begin_a(3)
    share(0)
    share(1)
    share(2)
    share(3)
    g_chain.turn_b(0)
    g_chain.turn_b(1)
    g_chain.turn_b(2)
    g_chain.turn_b(3)
    settle(0)
    settle(1)
    settle(2)
    settle(3)
    back.take_b(0)
    end_g(0)
    back.take_b(1)
    end_g(1)
    back.take_b(2)
    end_g(2)
    back.take_b(3)
    end_g(3)
    send_last()
    finish()
    ahead(0)
    ahead(3)
    ahead(1)
    ahead(2)
    w.drain()


def local(entity_table, phases, head_owner, head_row, relation, tail_ids, known_tails):
    messages = 16 + 63 + 24 + 4 + 24 + 12 + 60 + 8 + 1
    here = pl.BlockSpec(memory_space=VMEM)
    e, r = pl.pallas_call(
        step_kernel,
        out_shape=(jax.ShapeDtypeStruct((4, 2 * COLS), F32), jax.ShapeDtypeStruct((1024, COLS), WIRE)),
        in_specs=[pl.BlockSpec(memory_space=pltpu.HBM)] * 7,
        out_specs=[here, here],
        scratch_shapes=[
            pltpu.SemaphoreType.DMA((messages,)),
            pltpu.SemaphoreType.DMA((messages,)),
            pltpu.SemaphoreType.DMA((7,)),
            VMEM((LISTED, TRIPLES), jnp.int32),
            VMEM((1, TRIPLES), jnp.int32),
            VMEM((1, TRIPLES), jnp.int32),
            VMEM((1, TRIPLES), jnp.int32),
            VMEM((1, TRIPLES), jnp.int32),
            VMEM((1024, COLS), F32),
            VMEM((3, 1024, COLS), BF16),
            VMEM((TRIPLES, COLS), F32),
            VMEM((TRIPLES, COLS), F32),
            VMEM((TRIPLES, STEP), jnp.int32),
            VMEM((TRIPLES, 1024), BF16),
            VMEM((2, 1024, COLS), BF16),
            VMEM((8, 8, STEP), F32),
            VMEM((2, TRIPLES, COLS), BF16),
            VMEM((8, TRIPLES, STEP), BF16),
            VMEM((2, TRIPLES, COLS), BF16),
            VMEM((2, TRIPLES, COLS), BF16),
            VMEM((2, 1024, COLS), F32),
            VMEM((1024, COLS), F32),
            VMEM((1024, COLS), F32),
            VMEM((3, 4, 4, 16, COLS), WIRE),
            VMEM((3, 4, 4, 16, COLS), WIRE),
            VMEM((4, 4, 16, COLS), F32),
            VMEM((3, 4, 16, COLS), WIRE),
            VMEM((3, 4, 16, COLS), WIRE),
            VMEM((4, 16, COLS), F32),
            VMEM((4, 2, 8, COLS), F32),
            VMEM((8, COLS), F32),
            VMEM((8, COLS), F32),
            VMEM((3, 4, 4, 16, COLS), WIRE),
            VMEM((3, 4, 4, 16, COLS), WIRE),
            VMEM((4, 4, 16, COLS), F32),
            VMEM((3, 4, 16, COLS), WIRE),
            VMEM((3, 4, 16, COLS), WIRE),
            VMEM((4, 16, COLS), F32),
            VMEM((4, 4, 16, COLS), WIRE),
        ],
        compiler_params=pltpu.CompilerParams(collective_id=0, has_side_effects=True, vmem_limit_bytes=40 << 20),
        name="step",
    )(*(pltpu.with_memory_space_constraint(v, pltpu.HBM) for v in (
        known_tails.T, head_owner.reshape(1, TRIPLES), head_row.reshape(1, TRIPLES), relation.reshape(1, TRIPLES),
        tail_ids.reshape(1, TRIPLES), phases, entity_table)))
    return e, r.astype(F32)


def solution(mesh):
    in_specs = (
        P("ent", None),
        P("rel", None),
        P(("ent", "rel"), None),
        P(("ent", "rel")),
        P(("ent", "rel")),
        P(("ent", "rel")),
        P(("ent", "rel"), None),
    )
    out_specs = (P(("ent", "rel"), None), P("rel", None))
    return jax.shard_map(local, mesh=mesh, in_specs=in_specs, out_specs=out_specs, check_vma=False)
```
